128 devices in a mesh: segment: 2 (over z_hi), row: 8 (over y, core), col: 8 (over x, z_lo).
Axes of the slice: x: 4, y: 4, z: 4 (z_hi: 2, z_lo: 2; z = z_hi * 2 + z_lo), core: 2. Of those that a mesh axis runs over, the one named last changes fastest.
Arguments:
- dosage: float32 [2048, 12288], P(('segment', 'col'), 'row'), may hold values from 0 to 2, as said below
- missing: int32 [2048, 12288], P(('segment', 'col'), 'row'), may hold values 0 or 1
- residuals: bfloat16 [12288, 256], P('row'), may hold values from -6 to 6
- global_grm: bfloat16 [12288, 12288], P('row', 'col'), may hold values from -1 to 2
- seg_counts: int32 [6], replicated, may hold values from 1 to 1024, 2048 in all
Outputs:
- scores: bfloat16 [6, 12288, 256], P(None, ('row', 'col'), 'segment')
The draws below stay inside these ranges and needn't reach their ends.
Inputs may be any that keep to these rules, and one draw needn't show every extreme that they name: `dosage`: imputed alternative-allele dosages. 1 marks a missing genotype. `seg_counts`: SNP counts of the 6 segments, laid end to end over the 2048 variants; they sum to 2048 and the largest is exactly 1024.
All inputs are finite; a program needn't handle non-finite values. No bound on the sum of `missing` on one device may be relied on, other than what follows from the above.
Results may differ from the reference program's by a relative error of at most 0.0053.
Values may be sent and summed in bfloat16 or wider, within the bound.
A program may use at most 320 MiB of HBM per device.

```python
import math
import jax
import jax.numpy as jnp
import numpy as np
from jax import lax

TILE = 1536
RESCOLS = 256
MOST = 1024
SEGMENTS = 6
VARS = 2048
SAMPLES = 12288
N_SEGMENT = 2
N_ROW = 8


def draw_dosage(key, part):
    key_base, key_one, key_two, key_mix = jax.random.split(key, 4)
    base_freq = jax.random.uniform(key_base, (VARS, 1), jnp.float32, 0.05, 0.31)
    sample_pos = lax.broadcasted_iota(jnp.int32, (1, SAMPLES), 1).astype(jnp.float32)
    freq = base_freq * (1.0 + 2.0 * sample_pos / SAMPLES)
    first_allele = (jax.random.uniform(key_one, (VARS, SAMPLES), jnp.float32) < freq).astype(jnp.float32)
    second_allele = (jax.random.uniform(key_two, (VARS, SAMPLES), jnp.float32) < freq).astype(jnp.float32)
    genotype = first_allele + second_allele
    certainty = jax.random.uniform(key_mix, (VARS, SAMPLES), jnp.float32, 0.6, 1.0)
    return 2.0 * freq * (1.0 - certainty) + genotype * certainty


def draw_global_grm(key, part):
    spread_vals = jnp.clip(0.2 * jax.random.normal(key, (SAMPLES, SAMPLES), jnp.float32), -1.0, 1.0)
    on_diagonal = (lax.broadcasted_iota(jnp.int32, (SAMPLES, SAMPLES), 0) == lax.broadcasted_iota(jnp.int32, (SAMPLES, SAMPLES), 1)).astype(jnp.float32)
    return (spread_vals + on_diagonal).astype(jnp.bfloat16)


def set_ends(entries, own_key, smallest, top_value):
    longest = entries.shape.index(max(entries.shape))
    spots = []
    for shift in (0, 1):
        where = [jax.random.randint(jax.random.fold_in(own_key, axis), (), 0, length) for axis, length in enumerate(entries.shape)]
        where[longest] = (where[longest] + shift) % entries.shape[longest]
        spots.append(tuple(where))
    return entries.at[spots[0]].set(smallest).at[spots[1]].set(top_value)


def block_levels(own_key, extent, cuts, least, high):
    def one(position, shards_of):
        steps = jax.random.uniform(jax.random.fold_in(jax.random.fold_in(own_key, 6), position), (shards_of,), jnp.float32, least / len(cuts), high / len(cuts))
        return jnp.repeat(jnp.exp(steps), extent[position] // shards_of).reshape((-1,) + (1,) * (len(extent) - position - 1))

    level = one(*cuts[0])
    for cut in cuts[1:]:
        level = level * one(*cut)
    return level


def profile(count, total, most, slope):
    weights = [(1 << 20) // math.isqrt(standing ** slope) + 1 for standing in range(2, count + 1)]
    spare, given = total - most - (count - 1), [1] * (count - 1)
    while spare > 0:
        candidates = [i for i in range(count - 1) if given[i] < most]
        mass, budget = sum([weights[i] for i in candidates]), spare
        for i in candidates:
            more = min(most - given[i], max(1, budget * weights[i] // mass), spare)
            given[i] = given[i] + more
            spare = spare - more
    return np.array([most] + given)


def uneven(stream_key, number_of, total, bound, slope):
    if number_of == 2:
        one = jax.random.randint(stream_key, (), max(1, total - bound), min(bound, total - 1) + 1)
        return jnp.stack([one, total - one])
    tallies = jnp.asarray(profile(number_of, total, bound, slope), jnp.int32)
    couples = (number_of - 1) // 2
    source_of, receiver = tallies[1:1 + 2 * couples:2], tallies[2:2 + 2 * couples:2]
    slack = jnp.minimum(source_of - 1, bound - receiver)
    moved = jax.random.randint(jax.random.fold_in(stream_key, 1), (couples,), 0, 1 << 20) % (slack + 1)
    tallies = tallies.at[1:1 + 2 * couples:2].set(source_of - moved).at[2:2 + 2 * couples:2].set(receiver + moved)
    return tallies[jax.random.permutation(jax.random.fold_in(stream_key, 2), number_of)]


def bell_draw(stream_key, extent, width, most, shards=(), kind=jnp.bfloat16):
    entries = width * jax.random.normal(stream_key, extent, jnp.float32)
    if shards:
        entries = entries * block_levels(stream_key, extent, shards, -0.22, 0.18)
    return jnp.clip(entries, -most, most).astype(kind)


def setup_inputs(seed: int = 0) -> dict:
    arg_keys = jax.random.split(jax.random.key(seed), 6)
    return {
        "dosage": draw_dosage(jax.random.fold_in(arg_keys[5], 71), 0),
        "missing": set_ends((jax.random.randint(arg_keys[1], (VARS, SAMPLES), 0, 20) < 1).astype(jnp.int32), jax.random.fold_in(arg_keys[1], 1), 0, 1),
        "residuals": bell_draw(arg_keys[2], (SAMPLES, RESCOLS), 1.0, 6.0, ((0, 8),)),
        "global_grm": draw_global_grm(jax.random.fold_in(arg_keys[5], 71), 0),
        "seg_counts": uneven(arg_keys[4], SEGMENTS, VARS, MOST, 2).astype(jnp.int32),
    }


def reference(dosage, missing, residuals, global_grm, seg_counts):
    observed = (1 - missing).astype(jnp.float32)
    dosage_f = dosage.astype(jnp.float32)
    alt_count = lax.optimization_barrier(jnp.sum(dosage_f * observed, axis=1))
    obs_count = lax.optimization_barrier(jnp.sum(observed, axis=1))
    allele_freq = (alt_count + 1.0) / (2.0 * obs_count + 2.0)
    allele_spread = jnp.sqrt(2.0 * allele_freq * (1.0 - allele_freq))
    standard = (observed * (dosage_f - 2.0 * allele_freq[:, None]) / allele_spread[:, None]).astype(jnp.bfloat16)
    seg_starts = (jnp.cumsum(seg_counts) - seg_counts).astype(jnp.int32)
    shard_vars = VARS // N_SEGMENT
    res_f = residuals.astype(jnp.float32)
    outputs = []
    for segment_num in range(SEGMENTS):
        seg_start = seg_starts[segment_num]
        seg_count = seg_counts[segment_num]
        windows = []
        for shard_num in range(N_SEGMENT):
            lower = jnp.clip(seg_start, shard_num * shard_vars, (shard_num + 1) * shard_vars).astype(jnp.int32)
            upper = jnp.clip(seg_start + seg_count, shard_num * shard_vars, (shard_num + 1) * shard_vars).astype(jnp.int32)
            first_row = jnp.minimum(lower, VARS - MOST).astype(jnp.int32)
            window = lax.dynamic_slice_in_dim(standard, first_row, MOST, 0).astype(jnp.float32)
            var_index = first_row + jnp.arange(MOST, dtype=jnp.int32)
            keep_mask = (var_index >= lower) & (var_index < upper)
            windows.append(jnp.where(keep_mask[:, None], window, jnp.zeros_like(window)))

        def tile_rows(tile_num, windows=windows, seg_count=seg_count):
            row_start = (tile_num * TILE).astype(jnp.int32)
            grm_rows = lax.dynamic_slice_in_dim(global_grm, row_start, TILE, 0).astype(jnp.float32)
            total = jnp.zeros((TILE, RESCOLS), jnp.float32)
            for window in windows:
                rows_part = lax.dynamic_slice_in_dim(window, row_start, TILE, 1)
                local_gram = jnp.dot(rows_part.T, window, precision=lax.Precision.HIGHEST)
                hadamard = (local_gram / seg_count.astype(jnp.float32) * grm_rows).astype(jnp.bfloat16)
                total = total + jnp.dot(hadamard.astype(jnp.float32), res_f, precision=lax.Precision.HIGHEST)
            return total.astype(jnp.bfloat16)
        blocks = lax.map(tile_rows, jnp.arange(N_ROW, dtype=jnp.int32))
        outputs.append(blocks.reshape(SAMPLES, RESCOLS))
    return jnp.stack(outputs)
```

```python
import functools

import jax
import jax.numpy as jnp
from jax import lax
from jax.experimental import pallas as pl
from jax.experimental.pallas import tpu as pltpu
from jax.sharding import PartitionSpec as P

MESH_ID = pl.DeviceIdType.MESH
OWN = [(0, 0, 0), (0, 0, 2), (0, 0, 1), (0, 0, 3)]
ARRIVE = [
    (0, 1, 2), (1, 0, 0), (3, 0, 1),
    (0, 1, 3), (1, 0, 2), (3, 0, 3),
    (1, 0, 1), (3, 0, 0), (0, 1, 0),
    (1, 0, 3), (3, 0, 2), (0, 1, 1),
    (2, 0, 0), (2, 0, 1), (1, 1, 0),
    (1, 1, 2), (3, 1, 3), (3, 1, 1),
    (2, 0, 2), (2, 0, 3), (1, 1, 1),
    (1, 1, 3), (3, 1, 2), (3, 1, 0),
    (2, 1, 2), (2, 1, 3), (2, 1, 0), (2, 1, 1),
]
LAGS = {1: 11, 2: 16, 3: 21}
QROWS = 384


def piece_index(piece):
    dx, dz, q = piece
    return (dx * 2 + dz) * 4 + q


def gather_kernel(dosage, missing, resid, rows_out, cols_out, res_out,
                  turned, own, stat_mine, stat_in,
                  stat_send, stat_recv, own_sem, row_send, row_recv,
                  chain_send, chip_send, col_recv, res_send, res_recv):
    seg, row, col = lax.axis_index("segment"), lax.axis_index("row"), lax.axis_index("col")
    y, core = row // 2, row % 2
    x, zl = col // 2, col % 2
    samples = dosage.shape[1]
    col_of = lambda dx, dz: lax.rem(x + 4 - dx, 4) * 2 + lax.rem(zl + dz, 2)
    right = (seg, row, lax.rem(x + 1, 4) * 2 + zl)
    left = (seg, row, lax.rem(x + 3, 4) * 2 + zl)
    across = (seg, row, x * 2 + 1 - zl)
    up = (seg, lax.rem(y + 1, 4) * 2 + core, col)
    down = (seg, lax.rem(y + 3, 4) * 2 + core, col)
    mate = (seg, y * 2 + 1 - core, col)
    carries = core == zl
    place = lax.rem(y + 4 - x, 4)
    source = carries & (place == 0)
    takes = jnp.logical_not(source)

    barrier = pltpu.get_barrier_semaphore()
    peers = [(seg, lax.rem(row + d, 8), col) for d in range(1, 8)] + [right, left, across]
    for peer in peers:
        pl.semaphore_signal(barrier, inc=1, device_id=peer, device_id_type=MESH_ID)

    def turn(j, sums):
        lanes = pl.ds(pl.multiple_of(j * 128, 128), 128)
        tile = jnp.where(missing[:, lanes] == 0, dosage[:, lanes], -1.0).T
        turned[lanes, :] = tile
        seen = (tile >= 0.0).astype(jnp.float32).reshape(16, 8, 128)
        alt = jnp.maximum(tile, 0.0).reshape(16, 8, 128)
        return sums[0] + jnp.sum(alt, axis=0), sums[1] + jnp.sum(seen, axis=0)

    zero = jnp.zeros((8, 128), jnp.float32)
    alt, seen = lax.fori_loop(0, samples // 128, turn, (zero, zero))
    which = lax.broadcasted_iota(jnp.int32, (8, 128), 0)
    stat_mine[...] = jnp.where(which == 0, jnp.sum(alt, axis=0, keepdims=True),
                               jnp.sum(seen, axis=0, keepdims=True))

    pl.semaphore_wait(barrier, len(peers))

    def res_copy(half, target, n, src):
        part = pl.ds(half * (samples // 2), samples // 2)
        return pltpu.make_async_remote_copy(
            src_ref=src.at[part], dst_ref=res_out.at[part],
            send_sem=res_send.at[n], recv_sem=res_recv.at[half],
            device_id=target, device_id_type=MESH_ID)

    def stat_copy(d):
        return pltpu.make_async_remote_copy(
            src_ref=stat_mine, dst_ref=stat_in.at[d - 1],
            send_sem=stat_send.at[d - 1], recv_sem=stat_recv.at[d - 1],
            device_id=(seg, lax.rem(row + d, 8), col), device_id_type=MESH_ID)

    for d in range(1, 8):
        stat_copy(d).start()

    @pl.when(source)
    def _():
        res_copy(0, up, 0, resid).start()
        res_copy(1, down, 1, resid).start()
        res_copy(0, mate, 2, resid).start()
        res_copy(1, mate, 3, resid).start()

    total = stat_mine[...]
    for d in range(1, 8):
        stat_copy(d).wait_recv()
        total = total + stat_in[d - 1]
    alt, seen = total[0:1], total[1:2]
    freq = (alt + 1.0) / (2.0 * seen + 2.0)
    twice = 2.0 * freq
    scale = 1.0 / jnp.sqrt(twice * (1.0 - freq))

    def piece_rows(q):
        return pl.ds(q * QROWS, QROWS)

    def row_copy(n, piece, target, rel):
        dx, dz, q = piece
        c = col_of(dx, dz)
        src = own.at[piece_rows(q)] if (dx, dz) == (0, 0) else rows_out.at[c, piece_rows(q)]
        return pltpu.make_async_remote_copy(
            src_ref=src, dst_ref=rows_out.at[c, piece_rows(q)],
            send_sem=row_send.at[n], recv_sem=row_recv.at[piece_index(rel)],
            device_id=target, device_id_type=MESH_ID)

    def row_arrival(piece):
        dx, dz, q = piece
        dst = rows_out.at[col_of(dx, dz), piece_rows(q)]
        return pltpu.make_async_remote_copy(
            src_ref=dst, dst_ref=dst, send_sem=row_send.at[0],
            recv_sem=row_recv.at[piece_index(piece)], device_id=right, device_id_type=MESH_ID)

    sends = []

    def send_row(piece, where):
        dx, dz, q = piece
        if where == "right":
            target, rel = right, ((dx + 1) % 4, dz, q)
        elif where == "left":
            target, rel = left, ((dx + 3) % 4, dz, q)
        else:
            target, rel = across, (dx, 1 - dz, q)
        copy = row_copy(len(sends), piece, target, rel)
        copy.start()
        sends.append(copy)

    def col_ref(piece):
        dx, dz, q = piece
        return cols_out.at[col_of(dx, dz), piece_rows(q)]

    def chain_copy(piece, src, q):
        return pltpu.make_async_remote_copy(
            src_ref=src, dst_ref=col_ref(piece),
            send_sem=chain_send.at[piece_index(piece)], recv_sem=col_recv.at[piece_index(piece)],
            device_id=up if q < 2 else down, device_id_type=MESH_ID)

    def chip_copy(piece, src):
        return pltpu.make_async_remote_copy(
            src_ref=src, dst_ref=col_ref(piece),
            send_sem=chip_send.at[piece_index(piece)], recv_sem=col_recv.at[piece_index(piece)],
            device_id=mate, device_id_type=MESH_ID)

    def relays(q):
        last = 3 if q < 2 else 1
        return carries & (place != 0) & (place != last)

    def from_source(piece):
        dx, dz, q = piece
        src = own.at[piece_rows(q)] if (dx, dz) == (0, 0) else rows_out.at[col_of(dx, dz), piece_rows(q)]

        @pl.when(source)
        def _():
            chain_copy(piece, src, q).start()
            chip_copy(piece, src).start()

    def pass_on(piece, here):
        q = piece[2]
        last = 3 if q < 2 else 1
        chip_copy(piece, col_ref(piece)).wait_recv()
        if here != last:
            chain_copy(piece, col_ref(piece), q).start()
        chip_copy(piece, col_ref(piece)).start()

    def pass_res(half):
        @pl.when(carries & (place != 0))
        def _():
            res_copy(half, mate, 0, res_out).wait_recv()

            @pl.when(place != (3 if half == 0 else 1))
            def _():
                res_copy(half, up if half == 0 else down, half, res_out).start()
            res_copy(half, mate, 2 + half, res_out).start()

    def standardize(q):
        def tile(t, _):
            part = pl.ds(pl.multiple_of(q * QROWS + t * 128, 128), 128)
            v = turned[part, :]
            own[part, :] = jnp.where(v >= 0.0, (v - twice) * scale, 0.0).astype(jnp.bfloat16)
            return 0
        lax.fori_loop(0, QROWS // 128, tile, 0, unroll=True)

    for piece in OWN:
        standardize(piece[2])
    for piece in OWN:
        q = piece[2]
        from_source(piece)
        send_row(piece, "right")
        send_row((0, 0, (1, 0, 3, 2)[q]), "left")
        send_row((0, 0, (2, 3, 0, 1)[q]), "across")
    keep = pltpu.make_async_copy(own, rows_out.at[col], own_sem)
    keep.start()

    order = list(OWN) + list(ARRIVE)
    pass_res(0)
    pass_res(1)

    def chain_step(t):
        for here in (1, 2, 3):
            due = []
            for hops in (1, 2, 3):
                j = t - LAGS[hops]
                if 0 <= j < len(order) and (here if order[j][2] < 2 else 4 - here) == hops:
                    due.append(order[j])
            if t == len(OWN):
                for j in range(t):
                    hops = here if order[j][2] < 2 else 4 - here
                    if j + LAGS[hops] < t:
                        due.insert(0, order[j])
            if due:
                @pl.when(carries & (place == here))
                def _(due=due, here=here):
                    for piece in due:
                        pass_on(piece, here)

    for i, piece in enumerate(ARRIVE):
        dx, dz, q = piece
        row_arrival(piece).wait_recv()
        if (dx, dz) == (0, 1) and q >= 2:
            send_row(piece, "right" if q == 2 else "left")
            send_row(piece, "left" if q == 2 else "right")
        if dx == 1 and q in (0, 2) and (dz == 0 or q == 2):
            send_row(piece, "right")
        if dx == 3 and q in (1, 3) and (dz == 0 or q == 3):
            send_row(piece, "left")
        if dz == 0 and q < 2:
            send_row(piece, "across")
        from_source(piece)
        chain_step(i + len(OWN))
    for t in range(len(order), len(order) + LAGS[3]):
        chain_step(t)

    keep.wait()
    for copy in sends:
        copy.wait_send()
    for d in range(1, 8):
        stat_copy(d).wait_send()

    @pl.when(source)
    def _():
        for half in (0, 1):
            res_copy(half, up if half == 0 else down, half, resid).wait_send()
            res_copy(half, mate, 2 + half, resid).wait_send()
        for piece in order:
            q = piece[2]
            chain_copy(piece, col_ref(piece), q).wait_send()
            chip_copy(piece, col_ref(piece)).wait_send()

    @pl.when(carries & (place != 0))
    def _():
        for half in (0, 1):
            res_copy(half, mate, 2 + half, res_out).wait_send()
        for piece in order:
            chip_copy(piece, col_ref(piece)).wait_send()

    for half in (0, 1):
        @pl.when(relays(0 if half == 0 else 2))
        def _(half=half):
            res_copy(half, up if half == 0 else down, half, res_out).wait_send()
            for piece in order:
                if (piece[2] >= 2) == (half == 1):
                    chain_copy(piece, col_ref(piece), piece[2]).wait_send()

    @pl.when(jnp.logical_not(carries))
    def _():
        for half in (0, 1):
            res_copy(half, mate, 0, res_out).wait_recv()
        for piece in order:
            chip_copy(piece, col_ref(piece)).wait_recv()


def gather(dosage, missing, residuals):
    variants, samples = dosage.shape
    tile = jax.ShapeDtypeStruct((8, samples, variants), jnp.bfloat16)
    vmem = pl.BlockSpec(memory_space=pltpu.VMEM)
    hbm = pl.BlockSpec(memory_space=pl.ANY)
    dma = pltpu.SemaphoreType.DMA
    return pl.pallas_call(
        gather_kernel,
        out_shape=(tile, tile, jax.ShapeDtypeStruct(residuals.shape, residuals.dtype)),
        in_specs=[vmem, vmem, hbm],
        out_specs=(hbm, hbm, hbm),
        scratch_shapes=[
            pltpu.VMEM((samples, variants), jnp.float32),
            pltpu.VMEM((samples, variants), jnp.bfloat16),
            pltpu.VMEM((8, 128), jnp.float32),
            pltpu.VMEM((7, 8, 128), jnp.float32),
            dma((7,)), dma((7,)), dma(()), dma((28,)), dma((32,)),
            dma((32,)), dma((32,)), dma((32,)), dma((4,)), dma((2,)),
        ],
        compiler_params=pltpu.CompilerParams(collective_id=1, has_side_effects=True),
        name="gather_genotypes",
    )(dosage, missing, residuals)


SLOTS = 5
DEPTH = 256
NT = (((1,), (1,)), ((), ()))


def scores_kernel(meta, inv, rows, rows_all, cols_all, grm, res_own, res_all, out,
                  cols, res, acc, sems):
    tiles = cols.shape[1] // 256

    @pl.when(pl.program_id(0) == 0)
    def _():
        def fetch(col_src, res_src):
            one = pltpu.make_async_copy(col_src, cols, sems.at[0])
            two = pltpu.make_async_copy(res_src, res, sems.at[1])
            one.start()
            two.start()
            one.wait()
            two.wait()

        pl.when(meta[2 * SLOTS] == 1)(lambda: fetch(rows_all, res_own))
        pl.when(meta[2 * SLOTS] == 0)(lambda: fetch(cols_all, res_all))

    def slot(k, carry):
        lower, upper = meta[2 * k], meta[2 * k + 1]
        first = lower // DEPTH
        blocks = jnp.where(upper > lower, (upper + DEPTH - 1) // DEPTH - first, 0)

        def with_blocks(count):
            left = []
            for i in range(count):
                block = jnp.concatenate(
                    [rows[2 * (first + i)], rows[2 * (first + i) + 1]], axis=1)
                variant = (first + i) * DEPTH + lax.broadcasted_iota(jnp.int32, block.shape, 1)
                keep = (variant >= lower) & (variant < upper)
                left.append(jnp.where(keep, block, jnp.zeros_like(block)))
            left = jnp.concatenate(left, axis=1)
            for t in range(tiles):
                part = pl.ds(t * 256, 256)
                right = jnp.concatenate(
                    [cols[2 * first + j, part, :] for j in range(2 * count)], axis=1)
                gram = lax.dot_general(left, right, NT, preferred_element_type=jnp.float32)
                hadamard = (gram * grm[:, part].astype(jnp.float32)).astype(jnp.bfloat16)
                term = jnp.dot(hadamard, res[part, :], preferred_element_type=jnp.float32)
                if t == 0:
                    acc[...] = term
                else:
                    acc[...] += term
            total = (acc[...] * inv[k]).astype(jnp.bfloat16)
            for j in range(out.shape[1]):
                for half in range(2):
                    out[half, j, k] = total[j * 192:(j + 1) * 192, half * 128:(half + 1) * 128]

        for count in range(1, 5):
            pl.when(blocks == count)(functools.partial(with_blocks, count))

        @pl.when(blocks == 0)
        def _():
            for j in range(out.shape[1]):
                for half in range(2):
                    out[half, j, k] = jnp.zeros((192, 128), out.dtype)

        return carry

    lax.fori_loop(0, SLOTS, slot, 0)


def local_scores(meta, inv, rows, cols, grm, res_own, res_all, step=768):
    samples = rows.shape[1]
    hbm = pl.BlockSpec(memory_space=pl.ANY)
    return pl.pallas_call(
        scores_kernel,
        out_shape=jax.ShapeDtypeStruct((2, 8, SLOTS, 192, 128), jnp.bfloat16),
        grid_spec=pltpu.PrefetchScalarGridSpec(
            num_scalar_prefetch=2, grid=(samples // step,),
            in_specs=[
                pl.BlockSpec((8, step, 128), lambda m, *_: (0, m, 0)),
                hbm, hbm,
                pl.BlockSpec((step, samples), lambda m, *_: (m, 0)),
                hbm, hbm,
            ],
            out_specs=pl.BlockSpec((2, step // 192, SLOTS, 192, 128), lambda m, *_: (0, m, 0, 0, 0)),
            scratch_shapes=[
                pltpu.VMEM((8, samples, 128), jnp.bfloat16),
                pltpu.VMEM(res_own.shape, res_own.dtype),
                pltpu.VMEM((step, 256), jnp.float32),
                pltpu.SemaphoreType.DMA((2,)),
            ],
        ),
        compiler_params=pltpu.CompilerParams(vmem_limit_bytes=60 << 20),
        name="local_scores",
    )(meta, inv, rows, rows, cols, grm, res_own, res_all)


SEGS = 6


def scatter_kernel(parts, out, from_x, from_z, mid_x, mid_z, last_z, last_x,
                   own_sem, one_send, one_recv, two_send, two_recv):
    seg, row, col = lax.axis_index("segment"), lax.axis_index("row"), lax.axis_index("col")
    x, zl = col // 2, col % 2
    z = seg * 2 + zl
    rows = out.shape[1] // 2
    top, low = pl.ds(0, rows), pl.ds(rows, rows)

    def at(to_x, to_z):
        return (to_z // 2, row, to_x * 2 + to_z % 2)

    def shifted(base, d):
        return lax.rem(base + d, 4)

    barrier = pltpu.get_barrier_semaphore()
    for d in (1, 2, 3):
        pl.semaphore_signal(barrier, inc=1, device_id=at(shifted(x, d), z), device_id_type=MESH_ID)
        pl.semaphore_signal(barrier, inc=1, device_id=at(x, shifted(z, d)), device_id_type=MESH_ID)
    pl.semaphore_wait(barrier, 6)

    def x_one(d, j):
        to_x, for_z = shifted(x, d), shifted(z, j)
        return pltpu.make_async_remote_copy(
            src_ref=parts.at[for_z // 2, to_x, for_z % 2, :, top],
            dst_ref=from_x.at[j % 4, x],
            send_sem=one_send.at[0, d - 1, j - 1], recv_sem=one_recv.at[0, d - 1, j - 1],
            device_id=at(to_x, z), device_id_type=MESH_ID)

    def z_one(d, j):
        to_z, for_x = shifted(z, d), shifted(x, j)
        return pltpu.make_async_remote_copy(
            src_ref=parts.at[to_z // 2, for_x, to_z % 2, :, low],
            dst_ref=from_z.at[j % 4, z],
            send_sem=one_send.at[1, d - 1, j - 1], recv_sem=one_recv.at[1, d - 1, j - 1],
            device_id=at(x, to_z), device_id_type=MESH_ID)

    def own_copy(axis, j):
        if axis == 0:
            for_z = shifted(z, j)
            src, dst = parts.at[for_z // 2, x, for_z % 2, :, top], from_x.at[j % 4, x]
        else:
            for_x = shifted(x, j)
            src, dst = parts.at[z // 2, for_x, z % 2, :, low], from_z.at[j % 4, z]
        return pltpu.make_async_copy(src, dst, own_sem.at[axis, j - 1])

    def x_two(j):
        to_z = shifted(z, j)
        return pltpu.make_async_remote_copy(
            src_ref=mid_x.at[j - 1], dst_ref=last_z.at[z],
            send_sem=two_send.at[0, j - 1], recv_sem=two_recv.at[0, j - 1],
            device_id=at(x, to_z), device_id_type=MESH_ID)

    def z_two(j):
        to_x = shifted(x, j)
        return pltpu.make_async_remote_copy(
            src_ref=mid_z.at[j - 1], dst_ref=last_x.at[x],
            send_sem=two_send.at[1, j - 1], recv_sem=two_recv.at[1, j - 1],
            device_id=at(to_x, z), device_id_type=MESH_ID)

    order = (2, 1, 3, 4)
    for j in order:
        own_copy(0, j).start()
        own_copy(1, j).start()
        for d in (2, 1, 3):
            x_one(d, j).start()
            z_one(d, j).start()

    f32 = jnp.float32
    for j in order:
        own_copy(0, j).wait()
        for d in (1, 2, 3):
            x_one(d, j).wait_recv()
        for k in range(SLOTS):
            got = [from_x[j % 4, i, k].astype(f32) for i in range(4)]
            total = ((got[0] + got[1]) + (got[2] + got[3])).astype(jnp.bfloat16)
            if j < 4:
                mid_x[j - 1, k] = total
            else:
                last_z[z, k] = total
        if j < 4:
            x_two(j).start()
        own_copy(1, j).wait()
        for d in (1, 2, 3):
            z_one(d, j).wait_recv()
        for s in range(SEGS):
            total = jnp.zeros((rows, 128), f32)
            if s < SLOTS:
                total = from_z[j % 4, 0, s].astype(f32) + from_z[j % 4, 1, s].astype(f32)
            if s > 0:
                total = total + (from_z[j % 4, 2, s - 1].astype(f32) + from_z[j % 4, 3, s - 1].astype(f32))
            total = total.astype(jnp.bfloat16)
            if j < 4:
                mid_z[j - 1, s] = total
            else:
                last_x[x, s] = total
        if j < 4:
            z_two(j).start()

    for j in (1, 2, 3):
        x_two(j).wait_recv()
        z_two(j).wait_recv()
    for s in range(SEGS):
        total = jnp.zeros((rows, 128), f32)
        if s < SLOTS:
            total = last_z[0, s].astype(f32) + last_z[1, s].astype(f32)
        if s > 0:
            total = total + (last_z[2, s - 1].astype(f32) + last_z[3, s - 1].astype(f32))
        out[s, top] = total.astype(jnp.bfloat16)
        got = [last_x[i, s].astype(f32) for i in range(4)]
        out[s, low] = ((got[0] + got[1]) + (got[2] + got[3])).astype(jnp.bfloat16)

    for j in order:
        for d in (1, 2, 3):
            x_one(d, j).wait_send()
            z_one(d, j).wait_send()
        if j < 4:
            x_two(j).wait_send()
            z_two(j).wait_send()


def scatter(parts):
    rows, lanes = parts.shape[-2:]
    parts = parts.reshape(2, 4, 2, SLOTS, rows, lanes)
    half = rows // 2
    bf16 = jnp.bfloat16
    dma = pltpu.SemaphoreType.DMA
    return pl.pallas_call(
        scatter_kernel,
        out_shape=jax.ShapeDtypeStruct((SEGS, rows, lanes), bf16),
        in_specs=[pl.BlockSpec(memory_space=pl.ANY)],
        out_specs=pl.BlockSpec(memory_space=pltpu.VMEM),
        scratch_shapes=[
            pltpu.VMEM((4, 4, SLOTS, half, lanes), bf16),
            pltpu.VMEM((4, 4, SLOTS, half, lanes), bf16),
            pltpu.VMEM((3, SLOTS, half, lanes), bf16),
            pltpu.VMEM((3, SEGS, half, lanes), bf16),
            pltpu.VMEM((4, SLOTS, half, lanes), bf16),
            pltpu.VMEM((4, SEGS, half, lanes), bf16),
            dma((2, 4)), dma((2, 3, 4)), dma((2, 3, 4)), dma((2, 3)), dma((2, 3)),
        ],
        compiler_params=pltpu.CompilerParams(collective_id=2, has_side_effects=True),
        name="scatter_scores",
    )(parts)


def shards(dosage, missing, residuals, global_grm, seg_counts):
    seg, row, col = lax.axis_index("segment"), lax.axis_index("row"), lax.axis_index("col")
    shard_vars = 8 * dosage.shape[0]
    ends = jnp.cumsum(seg_counts) - seg * shard_vars
    starts = ends - seg_counts
    near = lambda v: lax.dynamic_slice_in_dim(v, seg, SLOTS, 0)
    lower = near(jnp.clip(starts, 0, shard_vars))
    upper = near(jnp.clip(ends, 0, shard_vars))
    bounds = jnp.stack([lower, upper], axis=1).reshape(-1)
    meta = jnp.concatenate([bounds, (row == col).astype(jnp.int32)[None]]).astype(jnp.int32)
    inv = 1.0 / near(seg_counts).astype(jnp.float32)
    rows, cols, res = gather(dosage, missing, residuals)
    parts = local_scores(meta, inv, rows, cols, global_grm, residuals, res)
    return scatter(parts)


def solution(mesh):
    placed = (
        P(("segment", "col"), "row"),
        P(("segment", "col"), "row"),
        P("row", None),
        P("row", "col"),
        P(),
    )
    return jax.shard_map(
        shards,
        mesh=mesh,
        in_specs=placed,
        out_specs=P(None, ("row", "col"), "segment"),
        check_vma=False,
    )
```

```python
import functools

import jax
import jax.numpy as jnp
from jax import lax
from jax.experimental import pallas as pl
from jax.experimental.pallas import tpu as pltpu
from jax.sharding import PartitionSpec as P

MESH_ID = pl.DeviceIdType.MESH
OWN = [(0, 0, 0), (0, 0, 2), (0, 0, 1), (0, 0, 3)]
ARRIVE = [
    (0, 1, 2), (1, 0, 0), (3, 0, 1),
    (0, 1, 3), (1, 0, 2), (3, 0, 3),
    (1, 0, 1), (3, 0, 0), (0, 1, 0),
    (1, 0, 3), (3, 0, 2), (0, 1, 1),
    (2, 0, 0), (2, 0, 1), (1, 1, 0),
    (1, 1, 2), (3, 1, 3), (3, 1, 1),
    (2, 0, 2), (2, 0, 3), (1, 1, 1),
    (1, 1, 3), (3, 1, 2), (3, 1, 0),
    (2, 1, 2), (2, 1, 3), (2, 1, 0), (2, 1, 1),
]
LAGS = {0: 4, 1: 12, 2: 18, 3: 24}
RES_AT = (-8, -8, -6, -6)
QROWS = 384


RES = [(4, 0, 0), (4, 0, 2), (4, 0, 1), (4, 0, 3)]


def piece_index(piece):
    dx, dz, q = piece
    return (dx * 2 + dz) * 4 + q


def gather_kernel(dosage, missing, resid, rows_out, cols_out, res_out,
                  turned, own, stat_mine, stat_in,
                  stat_send, stat_recv, own_sem, row_send, row_recv,
                  chain_send, chip_send, col_recv):
    seg, row, col = lax.axis_index("segment"), lax.axis_index("row"), lax.axis_index("col")
    y, core = row // 2, row % 2
    x, zl = col // 2, col % 2
    samples = dosage.shape[1]
    col_of = lambda dx, dz: lax.rem(x + 4 - dx, 4) * 2 + lax.rem(zl + dz, 2)
    right = (seg, row, lax.rem(x + 1, 4) * 2 + zl)
    left = (seg, row, lax.rem(x + 3, 4) * 2 + zl)
    across = (seg, row, x * 2 + 1 - zl)
    up = (seg, lax.rem(y + 1, 4) * 2 + core, col)
    down = (seg, lax.rem(y + 3, 4) * 2 + core, col)
    mate = (seg, y * 2 + 1 - core, col)
    first = core == zl
    place = lax.rem(y + 4 - x, 4)
    source = first & (place == 0)
    helper = jnp.logical_not(first) & (place == 0)

    barrier = pltpu.get_barrier_semaphore()
    peers = [(seg, lax.rem(row + d, 8), col) for d in range(1, 8)] + [right, left, across]
    for peer in peers:
        pl.semaphore_signal(barrier, inc=1, device_id=peer, device_id_type=MESH_ID)

    def turn(j, sums):
        lanes = pl.ds(pl.multiple_of(j * 128, 128), 128)
        tile = jnp.where(missing[:, lanes] == 0, dosage[:, lanes], -1.0).T
        turned[lanes, :] = tile
        seen = (tile >= 0.0).astype(jnp.float32).reshape(16, 8, 128)
        alt = jnp.maximum(tile, 0.0).reshape(16, 8, 128)
        return sums[0] + jnp.sum(alt, axis=0), sums[1] + jnp.sum(seen, axis=0)

    zero = jnp.zeros((8, 128), jnp.float32)
    alt, seen = lax.fori_loop(0, samples // 128, turn, (zero, zero))
    which = lax.broadcasted_iota(jnp.int32, (8, 128), 0)
    stat_mine[...] = jnp.where(which == 0, jnp.sum(alt, axis=0, keepdims=True),
                               jnp.sum(seen, axis=0, keepdims=True))

    pl.semaphore_wait(barrier, len(peers))

    def piece_rows(q):
        return pl.ds(q * QROWS, QROWS)

    def col_ref(piece):
        dx, dz, q = piece
        if dx == 4:
            return res_out.at[piece_rows(q)]
        return cols_out.at[col_of(dx, dz), piece_rows(q)]

    def chain_copy(piece, src, q):
        return pltpu.make_async_remote_copy(
            src_ref=src, dst_ref=col_ref(piece),
            send_sem=chain_send.at[piece_index(piece)], recv_sem=col_recv.at[piece_index(piece)],
            device_id=up if q < 2 else down, device_id_type=MESH_ID)

    def chip_copy(piece, src):
        return pltpu.make_async_remote_copy(
            src_ref=src, dst_ref=col_ref(piece),
            send_sem=chip_send.at[piece_index(piece)], recv_sem=col_recv.at[piece_index(piece)],
            device_id=mate, device_id_type=MESH_ID)

    def from_source(piece):
        dx, dz, q = piece
        if dx == 4:
            src = resid.at[piece_rows(q)]
        else:
            here = (dx, dz) == (0, 0)
            src = own.at[piece_rows(q)] if here else rows_out.at[col_of(dx, dz), piece_rows(q)]

        @pl.when(source)
        def _():
            chip_copy(piece, src).start()
            if q % 2 == 0:
                chain_copy(piece, src, q).start()

    def stat_copy(d):
        return pltpu.make_async_remote_copy(
            src_ref=stat_mine, dst_ref=stat_in.at[d - 1],
            send_sem=stat_send.at[d - 1], recv_sem=stat_recv.at[d - 1],
            device_id=(seg, lax.rem(row + d, 8), col), device_id_type=MESH_ID)

    for d in range(1, 8):
        stat_copy(d).start()

    for piece in RES:
        from_source(piece)

    total = stat_mine[...]
    for d in range(1, 8):
        stat_copy(d).wait_recv()
        total = total + stat_in[d - 1]
    alt, seen = total[0:1], total[1:2]
    freq = (alt + 1.0) / (2.0 * seen + 2.0)
    twice = 2.0 * freq
    scale = 1.0 / jnp.sqrt(twice * (1.0 - freq))

    def row_copy(n, piece, target, rel):
        dx, dz, q = piece
        c = col_of(dx, dz)
        src = own.at[piece_rows(q)] if (dx, dz) == (0, 0) else rows_out.at[c, piece_rows(q)]
        return pltpu.make_async_remote_copy(
            src_ref=src, dst_ref=rows_out.at[c, piece_rows(q)],
            send_sem=row_send.at[n], recv_sem=row_recv.at[piece_index(rel)],
            device_id=target, device_id_type=MESH_ID)

    def row_arrival(piece):
        dx, dz, q = piece
        dst = rows_out.at[col_of(dx, dz), piece_rows(q)]
        return pltpu.make_async_remote_copy(
            src_ref=dst, dst_ref=dst, send_sem=row_send.at[0],
            recv_sem=row_recv.at[piece_index(piece)], device_id=right, device_id_type=MESH_ID)

    sends = []

    def send_row(piece, where):
        dx, dz, q = piece
        if where == "right":
            target, rel = right, ((dx + 1) % 4, dz, q)
        elif where == "left":
            target, rel = left, ((dx + 3) % 4, dz, q)
        else:
            target, rel = across, (dx, 1 - dz, q)
        copy = row_copy(len(sends), piece, target, rel)
        copy.start()
        sends.append(copy)

    def carrier(q):
        return first if q % 2 == 0 else jnp.logical_not(first)

    def pass_on(piece, here):
        q = piece[2]
        last = 3 if q < 2 else 1
        chip_copy(piece, col_ref(piece)).wait_recv()
        if here != last:
            chain_copy(piece, col_ref(piece), q).start()
        if here != 0:
            chip_copy(piece, col_ref(piece)).start()

    def standardize(q):
        def tile(t, _):
            part = pl.ds(pl.multiple_of(q * QROWS + t * 128, 128), 128)
            v = turned[part, :]
            own[part, :] = jnp.where(v >= 0.0, (v - twice) * scale, 0.0).astype(jnp.bfloat16)
            return 0
        lax.fori_loop(0, QROWS // 128, tile, 0, unroll=True)

    for piece in OWN:
        standardize(piece[2])
    for piece in OWN:
        q = piece[2]
        from_source(piece)
        send_row(piece, "right")
        send_row((0, 0, (1, 0, 3, 2)[q]), "left")
        send_row((0, 0, (2, 3, 0, 1)[q]), "across")
    keep = pltpu.make_async_copy(own, rows_out.at[col], own_sem)
    keep.start()

    order = RES + OWN + ARRIVE
    timed = list(zip(RES_AT, RES)) + list(enumerate(OWN + ARRIVE))

    def chain_step(t):
        for parity in (0, 1):
            for here in (0, 1, 2, 3):
                due = []
                for j, piece in timed:
                    if piece[2] % 2 != parity or (here == 0 and parity == 0):
                        continue
                    hops = here if piece[2] < 2 else (4 - here) % 4
                    if max(j + LAGS[hops], len(OWN)) == t:
                        due.append(piece)
                if due:
                    @pl.when(carrier(parity) & (place == here))
                    def _(due=due, here=here):
                        for piece in due:
                            pass_on(piece, here)

    for i, piece in enumerate(ARRIVE):
        dx, dz, q = piece
        row_arrival(piece).wait_recv()
        if (dx, dz) == (0, 1) and q >= 2:
            send_row(piece, "right" if q == 2 else "left")
            send_row(piece, "left" if q == 2 else "right")
        if dx == 1 and q in (0, 2) and (dz == 0 or q == 2):
            send_row(piece, "right")
        if dx == 3 and q in (1, 3) and (dz == 0 or q == 3):
            send_row(piece, "left")
        if dz == 0 and q < 2:
            send_row(piece, "across")
        from_source(piece)
        chain_step(i + len(OWN))
    for t in range(len(OWN + ARRIVE), len(OWN + ARRIVE) + LAGS[3]):
        chain_step(t)

    keep.wait()
    for copy in sends:
        copy.wait_send()
    for d in range(1, 8):
        stat_copy(d).wait_send()

    @pl.when(source)
    def _():
        for piece in order:
            chip_copy(piece, col_ref(piece)).wait_send()
            if piece[2] % 2 == 0:
                chain_copy(piece, col_ref(piece), piece[2]).wait_send()

    @pl.when(helper)
    def _():
        for piece in order:
            if piece[2] % 2 == 0:
                chip_copy(piece, col_ref(piece)).wait_recv()
            else:
                chain_copy(piece, col_ref(piece), piece[2]).wait_send()

    for q in range(4):
        mine = [piece for piece in order if piece[2] == q]
        last = 3 if q < 2 else 1

        @pl.when(carrier(q) & (place != 0))
        def _(mine=mine):
            for piece in mine:
                chip_copy(piece, col_ref(piece)).wait_send()

        @pl.when(carrier(q) & (place != 0) & (place != last))
        def _(mine=mine):
            for piece in mine:
                chain_copy(piece, col_ref(piece), piece[2]).wait_send()

        @pl.when(jnp.logical_not(carrier(q)) & (place != 0))
        def _(mine=mine):
            for piece in mine:
                chip_copy(piece, col_ref(piece)).wait_recv()


def gather(dosage, missing, residuals):
    variants, samples = dosage.shape
    tile = jax.ShapeDtypeStruct((8, samples, variants), jnp.bfloat16)
    vmem = pl.BlockSpec(memory_space=pltpu.VMEM)
    hbm = pl.BlockSpec(memory_space=pl.ANY)
    dma = pltpu.SemaphoreType.DMA
    return pl.pallas_call(
        gather_kernel,
        out_shape=(tile, tile, jax.ShapeDtypeStruct(residuals.shape, residuals.dtype)),
        in_specs=[vmem, vmem, hbm],
        out_specs=(hbm, hbm, hbm),
        scratch_shapes=[
            pltpu.VMEM((samples, variants), jnp.float32),
            pltpu.VMEM((samples, variants), jnp.bfloat16),
            pltpu.VMEM((8, 128), jnp.float32),
            pltpu.VMEM((7, 8, 128), jnp.float32),
            dma((7,)), dma((7,)), dma(()), dma((28,)), dma((32,)),
            dma((36,)), dma((36,)), dma((36,)),
        ],
        compiler_params=pltpu.CompilerParams(collective_id=1, has_side_effects=True),
        name="gather_genotypes",
    )(dosage, missing, residuals)


SLOTS = 5
SEGS = 6
DEPTH = 256
STEPS = 8
XO = (2, 1, 3, 0)


def scores_kernel(counts, rows_all, cols_all, grm_all, res_own, res_all, out,
                  rows, cols, wide, grm, res, acc, parts, from_x, from_z, mid_x, mid_z, last_z, last_x,
                  plan, load_sem, one_send, one_recv, two_send, two_recv):
    seg, row, col = (lax.axis_index(a) for a in ("segment", "row", "col"))
    x, zl = col // 2, col % 2
    z = seg * 2 + zl
    f32, bf16 = jnp.float32, jnp.bfloat16
    samples = cols.shape[1]
    shard = cols.shape[0] * cols.shape[2]
    chunk = samples // 4
    half = out.shape[1] // 2
    top, low = pl.ds(0, half), pl.ds(half, half)

    def at(to_x, to_z):
        return (to_z // 2, row, to_x * 2 + to_z % 2)

    def shifted(base, d):
        return lax.rem(base + d, 4)

    barrier = pltpu.get_barrier_semaphore()
    for d in (1, 2, 3):
        pl.semaphore_signal(barrier, inc=1, device_id=at(shifted(x, d), z), device_id_type=MESH_ID)
        pl.semaphore_signal(barrier, inc=1, device_id=at(x, shifted(z, d)), device_id_type=MESH_ID)

    def load(n, src, dst):
        return pltpu.make_async_copy(src, dst, load_sem.at[n])

    def chunk_rows(t):
        return pl.ds(pl.multiple_of(shifted(x, XO[t]) * chunk, chunk), chunk)

    def row_load(t):
        return load(2 + t, rows_all.at[:, chunk_rows(t)], rows.at[t])

    def grm_load(t):
        return load(6 + t, grm_all.at[chunk_rows(t)], grm.at[t])

    diagonal = row == col

    @pl.when(diagonal)
    def _():
        load(0, rows_all, cols).start()
        load(1, res_own, res).start()

    @pl.when(jnp.logical_not(diagonal))
    def _():
        load(0, cols_all, cols).start()
        load(1, res_all, res).start()

    for t in range(4):
        row_load(t).start()
        grm_load(t).start()

    flip = seg == 1
    sizes = [jnp.where(flip, counts[SEGS - 1 - i], counts[i]) for i in range(SLOTS)]
    ends, total = [], jnp.int32(0)
    for size in sizes:
        total = total + size
        ends.append(jnp.minimum(total, shard))
    pos, k = jnp.int32(0), jnp.int32(0)
    for j in range(STEPS):
        end, size = ends[SLOTS - 1], sizes[SLOTS - 1]
        for i in range(SLOTS - 2, -1, -1):
            end = jnp.where(k <= i, ends[i], end)
            size = jnp.where(k <= i, sizes[i], size)
        block = jnp.minimum(pos // DEPTH, shard // DEPTH - 1)
        stop = jnp.maximum(jnp.minimum(end, (block + 1) * DEPTH), pos)
        plan[0, j] = jnp.where(flip, shard // DEPTH - 1 - block, block)
        plan[1, j] = jnp.where(flip, shard - stop, pos)
        plan[2, j] = jnp.where(flip, shard - pos, stop)
        plan[3, j] = k
        plan[4, j] = size
        k = jnp.where(stop == end, k + 1, k)
        pos = stop

    load(0, cols_all, cols).wait()

    def widen(b, carry):
        wide[b, 0:128, :] = cols[2 * b].T
        wide[b, 128:256, :] = cols[2 * b + 1].T
        return carry

    lax.fori_loop(0, shard // DEPTH, widen, 0)
    load(1, res_all, res).wait()
    for t in range(4):
        row_load(t).wait()
    pl.semaphore_wait(barrier, 6)

    def compute(t, carry):
        acc[...] = jnp.zeros_like(acc)
        for j in range(STEPS):
            block, lower, upper = plan[0, j], plan[1, j], plan[2, j]
            left = jnp.concatenate([rows[t, 2 * block], rows[t, 2 * block + 1]], axis=1)
            variant = block * DEPTH + lax.broadcasted_iota(jnp.int32, left.shape, 1)
            left = jnp.where((variant >= lower) & (variant < upper), left, jnp.zeros_like(left))
            term = None
            for n in range(samples // 256):
                part = pl.ds(n * 256, 256)
                gram = jnp.dot(left, wide[block, :, part], preferred_element_type=f32)
                hadamard = (gram * grm[t, :, part].astype(f32)).astype(bf16)
                new = jnp.dot(hadamard, res[part, :], preferred_element_type=f32)
                term = new if term is None else term + new
            scale = 1.0 / jnp.full((1, 256), plan[4, j], jnp.int32).astype(f32)
            term = term * scale
            for k in range(max(0, j - 3), min(j, SLOTS - 1) + 1):
                acc[k] += jnp.where(plan[3, j] == k, term, 0.0)
        for k in range(SLOTS):
            for i in range(4):
                r = (i % 2) * 2 * half
                lanes = slice((i // 2) * 128, (i // 2) * 128 + 128)
                parts[t, i, k] = acc[k, r:r + 2 * half, lanes].astype(bf16)
        return carry

    def x_one(t, i):
        return pltpu.make_async_remote_copy(
            src_ref=parts.at[t, i, :, top], dst_ref=from_x.at[i, t],
            send_sem=one_send.at[0, t, i], recv_sem=one_recv.at[0, t, i],
            device_id=at(shifted(x, XO[t]), z), device_id_type=MESH_ID)

    def z_one(t, d):
        to_z = shifted(z, d)
        return pltpu.make_async_remote_copy(
            src_ref=parts.at[t, to_z, :, low], dst_ref=from_z.at[t, d - 1],
            send_sem=one_send.at[1, t, d], recv_sem=one_recv.at[1, t, d],
            device_id=at(x, to_z), device_id_type=MESH_ID)

    def x_two(d):
        to_z = shifted(z, d)
        return pltpu.make_async_remote_copy(
            src_ref=mid_x.at[to_z], dst_ref=last_z.at[d - 1],
            send_sem=two_send.at[0, d], recv_sem=two_recv.at[0, d],
            device_id=at(x, to_z), device_id_type=MESH_ID)

    def z_two(t):
        return pltpu.make_async_remote_copy(
            src_ref=mid_z.at[t], dst_ref=last_x.at[t],
            send_sem=two_send.at[1, t], recv_sem=two_recv.at[1, t],
            device_id=at(shifted(x, XO[t]), z), device_id_type=MESH_ID)

    def place_slots(write, mine, others):
        def go(near, far, seg_is):
            for s in range(SEGS):
                total = jnp.zeros((half, 128), f32)
                i = s if seg_is == 0 else SEGS - 1 - s
                if i < SLOTS:
                    total = total + (mine(i) + others(near, i))
                if SEGS - 1 - i < SLOTS:
                    total = total + (others(far, SEGS - 1 - i) + others(2, SEGS - 1 - i))
                write(s, total)

        for seg_is in (0, 1):
            for zl_is in (0, 1):
                near, far = (3, 1) if zl_is == 0 else (1, 3)

                @pl.when((seg == seg_is) & (zl == zl_is))
                def _(near=near, far=far, seg_is=seg_is):
                    go(near, far, seg_is)

    def low_sum(t):
        for d in (1, 2, 3):
            z_one(t, d).wait_recv()

        def write(s, total):
            mid_z[t, s] = total.astype(bf16)

        place_slots(write, lambda i: parts[t, z, i, low, :].astype(f32),
                    lambda d, i: from_z[t, d - 1, i].astype(f32))
        if XO[t] != 0:
            z_two(t).start()

    for t in range(4):
        grm_load(t).wait()
        compute(t, 0)
        for i in (1, 2, 3, 0):
            if XO[t] != 0:
                x_one(t, i).start()
        for d in (2, 1, 3):
            z_one(t, d).start()
        if t > 0:
            low_sum(t - 1)

    def top_sum(i):
        for t in range(3):
            x_one(t, i).wait_recv()
        for k in range(SLOTS):
            got = [from_x[i, t, k].astype(f32) for t in range(3)]
            total = (got[0] + got[1]) + (got[2] + parts[3, i, k, top, :].astype(f32))
            mid_x[i, k] = total.astype(bf16)

    for i in range(4):
        top_sum(i)
    for d in (2, 1, 3):
        x_two(d).start()
    low_sum(3)
    for t in range(3):
        z_two(t).wait_recv()
    for s in range(SEGS):
        got = [last_x[t, s].astype(f32) for t in range(3)]
        out[s, low] = ((got[0] + got[1]) + (got[2] + mid_z[3, s].astype(f32))).astype(bf16)
    for d in (1, 2, 3):
        x_two(d).wait_recv()

    def write(s, total):
        out[s, top] = total.astype(bf16)

    place_slots(write, lambda i: mid_x[z, i].astype(f32), lambda d, i: last_z[d - 1, i].astype(f32))

    for t in range(4):
        if XO[t] != 0:
            for i in range(4):
                x_one(t, i).wait_send()
            z_two(t).wait_send()
        for d in (1, 2, 3):
            z_one(t, d).wait_send()
    for d in (1, 2, 3):
        x_two(d).wait_send()


def scores(seg_counts, rows, cols, grm, res_own, res_all):
    samples = rows.shape[1]
    out_rows = samples // 8
    half = out_rows // 2
    bf16 = jnp.bfloat16
    dma = pltpu.SemaphoreType.DMA
    hbm = pl.BlockSpec(memory_space=pl.ANY)
    return pl.pallas_call(
        scores_kernel,
        out_shape=jax.ShapeDtypeStruct((SEGS, out_rows, 128), bf16),
        in_specs=[pl.BlockSpec(memory_space=pltpu.SMEM), hbm, hbm, hbm, hbm, hbm],
        out_specs=pl.BlockSpec(memory_space=pltpu.VMEM),
        scratch_shapes=[
            pltpu.VMEM((4, 8, samples // 4, 128), bf16),
            pltpu.VMEM((8, samples, 128), bf16),
            pltpu.VMEM((4, DEPTH, samples), bf16),
            pltpu.VMEM((4, samples // 4, samples), bf16),
            pltpu.VMEM(res_own.shape, bf16),
            pltpu.VMEM((SLOTS, samples // 4, 256), jnp.float32),
            pltpu.VMEM((4, 4, SLOTS, out_rows, 128), bf16),
            pltpu.VMEM((4, 3, SLOTS, half, 128), bf16),
            pltpu.VMEM((4, 3, SLOTS, half, 128), bf16),
            pltpu.VMEM((4, SLOTS, half, 128), bf16),
            pltpu.VMEM((4, SEGS, half, 128), bf16),
            pltpu.VMEM((3, SLOTS, half, 128), bf16),
            pltpu.VMEM((3, SEGS, half, 128), bf16),
            pltpu.SMEM((5, STEPS), jnp.int32),
            dma((10,)), dma((2, 4, 4)), dma((2, 4, 4)), dma((2, 4)), dma((2, 4)),
        ],
        compiler_params=pltpu.CompilerParams(
            vmem_limit_bytes=60 << 20, collective_id=2, has_side_effects=True),
        name="scores",
    )(seg_counts, rows, cols, grm, res_own, res_all)


def shards(dosage, missing, residuals, global_grm, seg_counts):
    rows, cols, res = gather(dosage, missing, residuals)
    return scores(seg_counts, rows, cols, global_grm, residuals, res)


def solution(mesh):
    placed = (
        P(("segment", "col"), "row"),
        P(("segment", "col"), "row"),
        P("row", None),
        P("row", "col"),
        P(),
    )
    return jax.shard_map(
        shards,
        mesh=mesh,
        in_specs=placed,
        out_specs=P(None, ("row", "col"), "segment"),
        check_vma=False,
    )
```

```python
import functools

import jax
import jax.numpy as jnp
from jax import lax
from jax.experimental import pallas as pl
from jax.experimental.pallas import tpu as pltpu
from jax.sharding import PartitionSpec as P

MESH_ID = pl.DeviceIdType.MESH
OWN = [(0, 0, 0), (0, 0, 2), (0, 0, 1), (0, 0, 3)]
ARRIVE = [
    (0, 1, 2), (1, 0, 0), (3, 0, 1), (1, 0, 2), (3, 0, 3), (0, 1, 0),
    (0, 1, 3), (1, 0, 1), (3, 0, 0), (1, 0, 3), (3, 0, 2), (0, 1, 1),
    (1, 1, 0), (1, 1, 2), (3, 1, 2), (2, 0, 0), (2, 0, 1), (3, 1, 1),
    (2, 0, 2), (2, 0, 3), (1, 1, 1), (3, 1, 0), (3, 1, 3), (1, 1, 3),
    (2, 1, 2), (2, 1, 0), (2, 1, 1), (2, 1, 3),
]
CHAIN = {
    (0, 1): [
        (4, 4, 0, 1), (4, 4, 0, 3), (4, 0, 0, 1), (4, 0, 0, 3), (6, 3, 0, 1), (9, 3, 0, 3),
        (12, 0, 1, 3), (12, 1, 0, 1), (15, 1, 0, 3), (15, 0, 1, 1), (21, 3, 1, 1), (21, 2, 0, 1),
        (25, 2, 0, 3), (27, 1, 1, 1), (27, 3, 1, 3), (27, 1, 1, 3), (31, 2, 1, 1), (31, 2, 1, 3),
    ],
    (1, 0): [
        (4, 4, 0, 0), (4, 0, 0, 0), (12, 1, 0, 0), (18, 0, 1, 0), (21, 3, 0, 0), (21, 4, 0, 2),
        (21, 0, 0, 2), (25, 1, 1, 0), (27, 2, 0, 0), (27, 0, 1, 2), (30, 3, 1, 0), (31, 1, 0, 2),
        (31, 2, 1, 0), (31, 3, 0, 2), (31, 1, 1, 2), (31, 3, 1, 2), (31, 2, 0, 2), (31, 2, 1, 2),
    ],
    (1, 1): [
        (12, 4, 0, 1), (15, 0, 0, 1), (15, 3, 0, 1), (21, 1, 0, 1), (23, 0, 1, 1), (27, 3, 1, 1),
        (28, 4, 0, 3), (29, 2, 0, 1), (29, 0, 0, 3), (30, 3, 0, 3), (31, 1, 1, 1), (31, 0, 1, 3),
        (31, 1, 0, 3), (31, 2, 1, 1), (31, 2, 0, 3), (31, 3, 1, 3), (31, 1, 1, 3), (31, 2, 1, 3),
    ],
    (2, 0): [
        (12, 4, 0, 0), (12, 4, 0, 2), (15, 0, 0, 0), (15, 0, 0, 2), (21, 0, 1, 2), (21, 1, 0, 0),
        (24, 1, 0, 2), (25, 0, 1, 0), (27, 3, 0, 0), (28, 3, 0, 2), (31, 2, 0, 0), (31, 3, 1, 2),
        (31, 1, 1, 0), (31, 1, 1, 2), (31, 2, 0, 2), (31, 3, 1, 0), (31, 2, 1, 0), (31, 2, 1, 2),
    ],
    (2, 1): [
        (21, 4, 0, 1), (21, 4, 0, 3), (21, 0, 0, 1), (21, 0, 0, 3), (25, 3, 0, 1), (27, 3, 0, 3),
        (27, 0, 1, 3), (29, 1, 0, 1), (30, 1, 0, 3), (31, 0, 1, 1), (31, 3, 1, 1), (31, 2, 0, 3),
        (31, 2, 0, 1), (31, 3, 1, 3), (31, 1, 1, 1), (31, 1, 1, 3), (31, 2, 1, 1), (31, 2, 1, 3),
    ],
    (3, 0): [
        (4, 4, 0, 2), (4, 0, 0, 2), (12, 0, 1, 2), (15, 1, 0, 2), (21, 4, 0, 0), (21, 3, 0, 2),
        (21, 0, 0, 0), (25, 1, 1, 2), (27, 3, 1, 2), (27, 1, 0, 0), (29, 2, 0, 2), (31, 0, 1, 0),
        (31, 3, 0, 0), (31, 2, 1, 2), (31, 2, 0, 0), (31, 1, 1, 0), (31, 3, 1, 0), (31, 2, 1, 0),
    ],
    (3, 1): [
        (12, 4, 0, 3), (15, 0, 0, 3), (18, 3, 0, 3), (21, 0, 1, 3), (23, 1, 0, 3), (28, 4, 0, 1),
        (29, 0, 0, 1), (30, 2, 0, 3), (31, 3, 0, 1), (31, 3, 1, 3), (31, 1, 1, 3), (31, 1, 0, 1),
        (31, 0, 1, 1), (31, 2, 1, 3), (31, 3, 1, 1), (31, 2, 0, 1), (31, 1, 1, 1), (31, 2, 1, 1),
    ],
}
QROWS = 384


RES = [(4, 0, 0), (4, 0, 2), (4, 0, 1), (4, 0, 3)]


def piece_index(piece):
    dx, dz, q = piece
    return (dx * 2 + dz) * 4 + q


def gather_kernel(dosage, missing, resid, rows_out, cols_out, res_out,
                  turned, own, stat_mine, stat_in,
                  stat_send, stat_recv, own_sem, row_send, row_recv,
                  chain_send, chip_send, col_recv):
    seg, row, col = lax.axis_index("segment"), lax.axis_index("row"), lax.axis_index("col")
    y, core = row // 2, row % 2
    x, zl = col // 2, col % 2
    samples = dosage.shape[1]
    col_of = lambda dx, dz: lax.rem(x + 4 - dx, 4) * 2 + lax.rem(zl + dz, 2)
    right = (seg, row, lax.rem(x + 1, 4) * 2 + zl)
    left = (seg, row, lax.rem(x + 3, 4) * 2 + zl)
    across = (seg, row, x * 2 + 1 - zl)
    up = (seg, lax.rem(y + 1, 4) * 2 + core, col)
    down = (seg, lax.rem(y + 3, 4) * 2 + core, col)
    mate = (seg, y * 2 + 1 - core, col)
    first = core == zl
    place = lax.rem(y + 4 - x, 4)
    source = first & (place == 0)
    helper = jnp.logical_not(first) & (place == 0)

    barrier = pltpu.get_barrier_semaphore()
    peers = [(seg, lax.rem(row + d, 8), col) for d in range(1, 8)] + [right, left, across]
    for peer in peers:
        pl.semaphore_signal(barrier, inc=1, device_id=peer, device_id_type=MESH_ID)

    def turn(j, sums):
        lanes = pl.ds(pl.multiple_of(j * 128, 128), 128)
        tile = jnp.where(missing[:, lanes] == 0, dosage[:, lanes], -1.0).T
        turned[lanes, :] = tile
        seen = (tile >= 0.0).astype(jnp.float32).reshape(16, 8, 128)
        alt = jnp.maximum(tile, 0.0).reshape(16, 8, 128)
        return sums[0] + jnp.sum(alt, axis=0), sums[1] + jnp.sum(seen, axis=0)

    zero = jnp.zeros((8, 128), jnp.float32)
    alt, seen = lax.fori_loop(0, samples // 128, turn, (zero, zero))
    which = lax.broadcasted_iota(jnp.int32, (8, 128), 0)
    stat_mine[...] = jnp.where(which == 0, jnp.sum(alt, axis=0, keepdims=True),
                               jnp.sum(seen, axis=0, keepdims=True))

    pl.semaphore_wait(barrier, len(peers))

    def piece_rows(q):
        return pl.ds(q * QROWS, QROWS)

    def col_ref(piece):
        dx, dz, q = piece
        if dx == 4:
            return res_out.at[piece_rows(q)]
        return cols_out.at[col_of(dx, dz), piece_rows(q)]

    def chain_copy(piece, src, q):
        return pltpu.make_async_remote_copy(
            src_ref=src, dst_ref=col_ref(piece),
            send_sem=chain_send.at[piece_index(piece)], recv_sem=col_recv.at[piece_index(piece)],
            device_id=up if q < 2 else down, device_id_type=MESH_ID)

    def chip_copy(piece, src):
        return pltpu.make_async_remote_copy(
            src_ref=src, dst_ref=col_ref(piece),
            send_sem=chip_send.at[piece_index(piece)], recv_sem=col_recv.at[piece_index(piece)],
            device_id=mate, device_id_type=MESH_ID)

    def from_source(piece):
        dx, dz, q = piece
        if dx == 4:
            src = resid.at[piece_rows(q)]
        else:
            here = (dx, dz) == (0, 0)
            src = own.at[piece_rows(q)] if here else rows_out.at[col_of(dx, dz), piece_rows(q)]

        @pl.when(source)
        def _():
            chip_copy(piece, src).start()
            if q % 2 == 0:
                chain_copy(piece, src, q).start()

    def stat_copy(d):
        return pltpu.make_async_remote_copy(
            src_ref=stat_mine, dst_ref=stat_in.at[d - 1],
            send_sem=stat_send.at[d - 1], recv_sem=stat_recv.at[d - 1],
            device_id=(seg, lax.rem(row + d, 8), col), device_id_type=MESH_ID)

    for d in range(1, 8):
        stat_copy(d).start()

    for piece in RES:
        from_source(piece)

    total = stat_mine[...]
    for d in range(1, 8):
        stat_copy(d).wait_recv()
        total = total + stat_in[d - 1]
    alt, seen = total[0:1], total[1:2]
    freq = (alt + 1.0) / (2.0 * seen + 2.0)
    twice = 2.0 * freq
    scale = 1.0 / jnp.sqrt(twice * (1.0 - freq))

    def row_copy(n, piece, target, rel):
        dx, dz, q = piece
        c = col_of(dx, dz)
        src = own.at[piece_rows(q)] if (dx, dz) == (0, 0) else rows_out.at[c, piece_rows(q)]
        return pltpu.make_async_remote_copy(
            src_ref=src, dst_ref=rows_out.at[c, piece_rows(q)],
            send_sem=row_send.at[n], recv_sem=row_recv.at[piece_index(rel)],
            device_id=target, device_id_type=MESH_ID)

    def row_arrival(piece):
        dx, dz, q = piece
        dst = rows_out.at[col_of(dx, dz), piece_rows(q)]
        return pltpu.make_async_remote_copy(
            src_ref=dst, dst_ref=dst, send_sem=row_send.at[0],
            recv_sem=row_recv.at[piece_index(piece)], device_id=right, device_id_type=MESH_ID)

    sends = []

    def send_row(piece, where):
        dx, dz, q = piece
        if where == "right":
            target, rel = right, ((dx + 1) % 4, dz, q)
        elif where == "left":
            target, rel = left, ((dx + 3) % 4, dz, q)
        else:
            target, rel = across, (dx, 1 - dz, q)
        copy = row_copy(len(sends), piece, target, rel)
        copy.start()
        sends.append(copy)

    def carrier(q):
        return first if q % 2 == 0 else jnp.logical_not(first)

    def pass_on(piece, here):
        q = piece[2]
        last = 3 if q < 2 else 1
        chip_copy(piece, col_ref(piece)).wait_recv()
        if here != last:
            chain_copy(piece, col_ref(piece), q).start()
        if here != 0:
            chip_copy(piece, col_ref(piece)).start()

    def standardize(q):
        def tile(t, _):
            part = pl.ds(pl.multiple_of(q * QROWS + t * 128, 128), 128)
            v = turned[part, :]
            own[part, :] = jnp.where(v >= 0.0, (v - twice) * scale, 0.0).astype(jnp.bfloat16)
            return 0
        lax.fori_loop(0, QROWS // 128, tile, 0, unroll=True)

    for piece in OWN:
        standardize(piece[2])
    for piece in OWN:
        q = piece[2]
        from_source(piece)
        send_row(piece, "right")
        send_row((0, 0, (1, 0, 3, 2)[q]), "left")
        send_row((0, 0, (2, 3, 0, 1)[q]), "across")
    keep = pltpu.make_async_copy(own, rows_out.at[col], own_sem)
    keep.start()

    order = RES + OWN + ARRIVE

    def chain_step(t):
        for (here, parity), steps in CHAIN.items():
            due = [tuple(entry[1:]) for entry in steps if entry[0] == t]
            if due:
                @pl.when(carrier(parity) & (place == here))
                def _(due=due, here=here):
                    for piece in due:
                        pass_on(piece, here)

    for i, piece in enumerate(ARRIVE):
        dx, dz, q = piece
        row_arrival(piece).wait_recv()
        if (dx, dz) == (0, 1) and q >= 2:
            send_row(piece, "right" if q == 2 else "left")
            send_row(piece, "left" if q == 2 else "right")
        if dx == 1 and q in (0, 2) and (dz == 0 or q == 2):
            send_row(piece, "right")
        if dx == 3 and q in (1, 3) and (dz == 0 or q == 3):
            send_row(piece, "left")
        if dz == 0 and q < 2:
            send_row(piece, "across")
        from_source(piece)
        chain_step(i + len(OWN))

    keep.wait()
    for copy in sends:
        copy.wait_send()
    for d in range(1, 8):
        stat_copy(d).wait_send()

    @pl.when(source)
    def _():
        for piece in order:
            chip_copy(piece, col_ref(piece)).wait_send()
            if piece[2] % 2 == 0:
                chain_copy(piece, col_ref(piece), piece[2]).wait_send()

    @pl.when(helper)
    def _():
        for piece in order:
            if piece[2] % 2 == 0:
                chip_copy(piece, col_ref(piece)).wait_recv()
            else:
                chain_copy(piece, col_ref(piece), piece[2]).wait_send()

    for q in range(4):
        mine = [piece for piece in order if piece[2] == q]
        last = 3 if q < 2 else 1

        @pl.when(carrier(q) & (place != 0))
        def _(mine=mine):
            for piece in mine:
                chip_copy(piece, col_ref(piece)).wait_send()

        @pl.when(carrier(q) & (place != 0) & (place != last))
        def _(mine=mine):
            for piece in mine:
                chain_copy(piece, col_ref(piece), piece[2]).wait_send()

        @pl.when(jnp.logical_not(carrier(q)) & (place != 0))
        def _(mine=mine):
            for piece in mine:
                chip_copy(piece, col_ref(piece)).wait_recv()


def gather(dosage, missing, residuals):
    variants, samples = dosage.shape
    tile = jax.ShapeDtypeStruct((8, samples, variants), jnp.bfloat16)
    vmem = pl.BlockSpec(memory_space=pltpu.VMEM)
    hbm = pl.BlockSpec(memory_space=pl.ANY)
    dma = pltpu.SemaphoreType.DMA
    return pl.pallas_call(
        gather_kernel,
        out_shape=(tile, tile, jax.ShapeDtypeStruct(residuals.shape, residuals.dtype)),
        in_specs=[vmem, vmem, hbm],
        out_specs=(hbm, hbm, hbm),
        scratch_shapes=[
            pltpu.VMEM((samples, variants), jnp.float32),
            pltpu.VMEM((samples, variants), jnp.bfloat16),
            pltpu.VMEM((8, 128), jnp.float32),
            pltpu.VMEM((7, 8, 128), jnp.float32),
            dma((7,)), dma((7,)), dma(()), dma((28,)), dma((32,)),
            dma((36,)), dma((36,)), dma((36,)),
        ],
        compiler_params=pltpu.CompilerParams(collective_id=1, has_side_effects=True),
        name="gather_genotypes",
    )(dosage, missing, residuals)


SLOTS = 5
SEGS = 6
DEPTH = 256
STEPS = 8
XO = (2, 1, 3, 0)


def scores_kernel(counts, rows_all, cols_all, grm_all, res_own, res_all, out,
                  rows, cols, wide, grm, res, acc, parts, from_x, from_z, mid_x, mid_z, last_z, last_x,
                  plan, load_sem, one_send, one_recv, two_send, two_recv):
    seg, row, col = (lax.axis_index(a) for a in ("segment", "row", "col"))
    x, zl = col // 2, col % 2
    z = seg * 2 + zl
    f32, bf16 = jnp.float32, jnp.bfloat16
    samples = cols.shape[1]
    shard = cols.shape[0] * cols.shape[2]
    chunk = samples // 4
    half = out.shape[1] // 2
    top, low = pl.ds(0, half), pl.ds(half, half)

    def at(to_x, to_z):
        return (to_z // 2, row, to_x * 2 + to_z % 2)

    def shifted(base, d):
        return lax.rem(base + d, 4)

    barrier = pltpu.get_barrier_semaphore()
    for d in (1, 2, 3):
        pl.semaphore_signal(barrier, inc=1, device_id=at(shifted(x, d), z), device_id_type=MESH_ID)
        pl.semaphore_signal(barrier, inc=1, device_id=at(x, shifted(z, d)), device_id_type=MESH_ID)

    def load(n, src, dst):
        return pltpu.make_async_copy(src, dst, load_sem.at[n])

    def chunk_rows(t):
        return pl.ds(pl.multiple_of(shifted(x, XO[t]) * chunk, chunk), chunk)

    def row_load(t):
        return load(2 + t, rows_all.at[:, chunk_rows(t)], rows.at[t])

    def grm_load(t):
        return load(6 + t, grm_all.at[chunk_rows(t)], grm.at[t])

    diagonal = row == col

    @pl.when(diagonal)
    def _():
        load(0, rows_all, cols).start()
        load(1, res_own, res).start()

    @pl.when(jnp.logical_not(diagonal))
    def _():
        load(0, cols_all, cols).start()
        load(1, res_all, res).start()

    for t in range(4):
        row_load(t).start()
        grm_load(t).start()

    flip = seg == 1
    sizes = [jnp.where(flip, counts[SEGS - 1 - i], counts[i]) for i in range(SLOTS)]
    ends, total = [], jnp.int32(0)
    for size in sizes:
        total = total + size
        ends.append(jnp.minimum(total, shard))
    pos, k = jnp.int32(0), jnp.int32(0)
    for j in range(STEPS):
        end, size = ends[SLOTS - 1], sizes[SLOTS - 1]
        for i in range(SLOTS - 2, -1, -1):
            end = jnp.where(k <= i, ends[i], end)
            size = jnp.where(k <= i, sizes[i], size)
        block = jnp.minimum(pos // DEPTH, shard // DEPTH - 1)
        stop = jnp.maximum(jnp.minimum(end, (block + 1) * DEPTH), pos)
        plan[0, j] = jnp.where(flip, shard // DEPTH - 1 - block, block)
        plan[1, j] = jnp.where(flip, shard - stop, pos)
        plan[2, j] = jnp.where(flip, shard - pos, stop)
        plan[3, j] = k
        plan[4, j] = size
        k = jnp.where(stop == end, k + 1, k)
        pos = stop

    load(0, cols_all, cols).wait()

    def widen(b, carry):
        wide[b, 0:128, :] = cols[2 * b].T
        wide[b, 128:256, :] = cols[2 * b + 1].T
        return carry

    lax.fori_loop(0, shard // DEPTH, widen, 0)
    load(1, res_all, res).wait()
    for t in range(4):
        row_load(t).wait()
    pl.semaphore_wait(barrier, 6)

    def compute(t, carry):
        acc[...] = jnp.zeros_like(acc)
        for j in range(STEPS):
            block, lower, upper = plan[0, j], plan[1, j], plan[2, j]
            left = jnp.concatenate([rows[t, 2 * block], rows[t, 2 * block + 1]], axis=1)
            variant = block * DEPTH + lax.broadcasted_iota(jnp.int32, left.shape, 1)
            left = jnp.where((variant >= lower) & (variant < upper), left, jnp.zeros_like(left))
            term = None
            for n in range(samples // 256):
                part = pl.ds(n * 256, 256)
                gram = jnp.dot(left, wide[block, :, part], preferred_element_type=f32)
                hadamard = (gram * grm[t, :, part].astype(f32)).astype(bf16)
                new = jnp.dot(hadamard, res[part, :], preferred_element_type=f32)
                term = new if term is None else term + new
            scale = 1.0 / jnp.full((1, 256), plan[4, j], jnp.int32).astype(f32)
            term = term * scale
            for k in range(max(0, j - 3), min(j, SLOTS - 1) + 1):
                acc[k] += jnp.where(plan[3, j] == k, term, 0.0)
        for k in range(SLOTS):
            for i in range(4):
                r = (i % 2) * 2 * half
                lanes = slice((i // 2) * 128, (i // 2) * 128 + 128)
                parts[t, i, k] = acc[k, r:r + 2 * half, lanes].astype(bf16)
        return carry

    def x_one(t, i):
        return pltpu.make_async_remote_copy(
            src_ref=parts.at[t, i, :, top], dst_ref=from_x.at[i, t],
            send_sem=one_send.at[0, t, i], recv_sem=one_recv.at[0, t, i],
            device_id=at(shifted(x, XO[t]), z), device_id_type=MESH_ID)

    def z_one(t, d):
        to_z = shifted(z, d)
        return pltpu.make_async_remote_copy(
            src_ref=parts.at[t, to_z, :, low], dst_ref=from_z.at[t, d - 1],
            send_sem=one_send.at[1, t, d], recv_sem=one_recv.at[1, t, d],
            device_id=at(x, to_z), device_id_type=MESH_ID)

    def x_two(d):
        to_z = shifted(z, d)
        return pltpu.make_async_remote_copy(
            src_ref=mid_x.at[to_z], dst_ref=last_z.at[d - 1],
            send_sem=two_send.at[0, d], recv_sem=two_recv.at[0, d],
            device_id=at(x, to_z), device_id_type=MESH_ID)

    def z_two(t):
        return pltpu.make_async_remote_copy(
            src_ref=mid_z.at[t], dst_ref=last_x.at[t],
            send_sem=two_send.at[1, t], recv_sem=two_recv.at[1, t],
            device_id=at(shifted(x, XO[t]), z), device_id_type=MESH_ID)

    def place_slots(write, mine, others):
        def go(near, far, seg_is):
            for s in range(SEGS):
                total = jnp.zeros((half, 128), f32)
                i = s if seg_is == 0 else SEGS - 1 - s
                if i < SLOTS:
                    total = total + (mine(i) + others(near, i))
                if SEGS - 1 - i < SLOTS:
                    total = total + (others(far, SEGS - 1 - i) + others(2, SEGS - 1 - i))
                write(s, total)

        for seg_is in (0, 1):
            for zl_is in (0, 1):
                near, far = (3, 1) if zl_is == 0 else (1, 3)

                @pl.when((seg == seg_is) & (zl == zl_is))
                def _(near=near, far=far, seg_is=seg_is):
                    go(near, far, seg_is)

    def low_sum(t):
        for d in (1, 2, 3):
            z_one(t, d).wait_recv()

        def write(s, total):
            mid_z[t, s] = total.astype(bf16)

        place_slots(write, lambda i: parts[t, z, i, low, :].astype(f32),
                    lambda d, i: from_z[t, d - 1, i].astype(f32))
        if XO[t] != 0:
            z_two(t).start()

    for t in range(4):
        grm_load(t).wait()
        compute(t, 0)
        for i in (1, 2, 3, 0):
            if XO[t] != 0:
                x_one(t, i).start()
        for d in (2, 1, 3):
            z_one(t, d).start()
        if t > 0:
            low_sum(t - 1)

    def top_sum(i):
        for t in range(3):
            x_one(t, i).wait_recv()
        for k in range(SLOTS):
            got = [from_x[i, t, k].astype(f32) for t in range(3)]
            total = (got[0] + got[1]) + (got[2] + parts[3, i, k, top, :].astype(f32))
            mid_x[i, k] = total.astype(bf16)

    for i in range(4):
        top_sum(i)
    for d in (2, 1, 3):
        x_two(d).start()
    low_sum(3)
    for t in range(3):
        z_two(t).wait_recv()
    for s in range(SEGS):
        got = [last_x[t, s].astype(f32) for t in range(3)]
        out[s, low] = ((got[0] + got[1]) + (got[2] + mid_z[3, s].astype(f32))).astype(bf16)
    for d in (1, 2, 3):
        x_two(d).wait_recv()

    def write(s, total):
        out[s, top] = total.astype(bf16)

    place_slots(write, lambda i: mid_x[z, i].astype(f32), lambda d, i: last_z[d - 1, i].astype(f32))

    for t in range(4):
        if XO[t] != 0:
            for i in range(4):
                x_one(t, i).wait_send()
            z_two(t).wait_send()
        for d in (1, 2, 3):
            z_one(t, d).wait_send()
    for d in (1, 2, 3):
        x_two(d).wait_send()


def scores(seg_counts, rows, cols, grm, res_own, res_all):
    samples = rows.shape[1]
    out_rows = samples // 8
    half = out_rows // 2
    bf16 = jnp.bfloat16
    dma = pltpu.SemaphoreType.DMA
    hbm = pl.BlockSpec(memory_space=pl.ANY)
    return pl.pallas_call(
        scores_kernel,
        out_shape=jax.ShapeDtypeStruct((SEGS, out_rows, 128), bf16),
        in_specs=[pl.BlockSpec(memory_space=pltpu.SMEM), hbm, hbm, hbm, hbm, hbm],
        out_specs=pl.BlockSpec(memory_space=pltpu.VMEM),
        scratch_shapes=[
            pltpu.VMEM((4, 8, samples // 4, 128), bf16),
            pltpu.VMEM((8, samples, 128), bf16),
            pltpu.VMEM((4, DEPTH, samples), bf16),
            pltpu.VMEM((4, samples // 4, samples), bf16),
            pltpu.VMEM(res_own.shape, bf16),
            pltpu.VMEM((SLOTS, samples // 4, 256), jnp.float32),
            pltpu.VMEM((4, 4, SLOTS, out_rows, 128), bf16),
            pltpu.VMEM((4, 3, SLOTS, half, 128), bf16),
            pltpu.VMEM((4, 3, SLOTS, half, 128), bf16),
            pltpu.VMEM((4, SLOTS, half, 128), bf16),
            pltpu.VMEM((4, SEGS, half, 128), bf16),
            pltpu.VMEM((3, SLOTS, half, 128), bf16),
            pltpu.VMEM((3, SEGS, half, 128), bf16),
            pltpu.SMEM((5, STEPS), jnp.int32),
            dma((10,)), dma((2, 4, 4)), dma((2, 4, 4)), dma((2, 4)), dma((2, 4)),
        ],
        compiler_params=pltpu.CompilerParams(
            vmem_limit_bytes=60 << 20, collective_id=2, has_side_effects=True),
        name="scores",
    )(seg_counts, rows, cols, grm, res_own, res_all)


def shards(dosage, missing, residuals, global_grm, seg_counts):
    rows, cols, res = gather(dosage, missing, residuals)
    return scores(seg_counts, rows, cols, global_grm, residuals, res)


def solution(mesh):
    placed = (
        P(("segment", "col"), "row"),
        P(("segment", "col"), "row"),
        P("row", None),
        P("row", "col"),
        P(),
    )
    return jax.shard_map(
        shards,
        mesh=mesh,
        in_specs=placed,
        out_specs=P(None, ("row", "col"), "segment"),
        check_vma=False,
    )
```

```python
import functools

import jax
import jax.numpy as jnp
from jax import lax
from jax.experimental import pallas as pl
from jax.experimental.pallas import tpu as pltpu
from jax.sharding import PartitionSpec as P

MESH_ID = pl.DeviceIdType.MESH
OWN = [(0, 0, 0), (0, 0, 2), (0, 0, 1), (0, 0, 3)]
ARRIVE = [
    (0, 1, 2), (1, 0, 0), (3, 0, 1), (1, 0, 2), (3, 0, 3), (0, 1, 0),
    (0, 1, 3), (1, 0, 1), (3, 0, 0), (1, 0, 3), (3, 0, 2), (0, 1, 1),
    (1, 1, 0), (1, 1, 2), (3, 1, 2), (2, 0, 0), (2, 0, 1), (3, 1, 1),
    (2, 0, 2), (2, 0, 3), (1, 1, 1), (3, 1, 0), (3, 1, 3), (1, 1, 3),
    (2, 1, 2), (2, 1, 0), (2, 1, 1), (2, 1, 3),
]
CHAIN = {
    (0, 1): [
        (4, 4, 0, 1), (4, 4, 0, 3), (4, 0, 0, 1), (4, 0, 0, 3), (6, 3, 0, 1), (9, 3, 0, 3),
        (12, 0, 1, 3), (12, 1, 0, 1), (15, 1, 0, 3), (15, 0, 1, 1), (21, 3, 1, 1), (21, 2, 0, 1),
        (25, 2, 0, 3), (27, 1, 1, 1), (27, 3, 1, 3), (27, 1, 1, 3), (31, 2, 1, 1), (31, 2, 1, 3),
    ],
    (1, 0): [
        (4, 4, 0, 0), (4, 0, 0, 0), (12, 1, 0, 0), (18, 0, 1, 0), (21, 3, 0, 0), (21, 4, 0, 2),
        (21, 0, 0, 2), (25, 1, 1, 0), (27, 2, 0, 0), (27, 0, 1, 2), (30, 3, 1, 0), (31, 1, 0, 2),
        (31, 2, 1, 2), (31, 3, 0, 2), (31, 2, 1, 0), (31, 1, 1, 2), (31, 3, 1, 2), (31, 2, 0, 2),
    ],
    (1, 1): [
        (12, 4, 0, 1), (15, 0, 0, 1), (15, 3, 0, 1), (21, 1, 0, 1), (23, 0, 1, 1), (27, 3, 1, 1),
        (28, 4, 0, 3), (29, 2, 0, 1), (29, 0, 0, 3), (30, 3, 0, 3), (31, 1, 1, 1), (31, 1, 1, 3),
        (31, 0, 1, 3), (31, 1, 0, 3), (31, 2, 1, 1), (31, 2, 1, 3), (31, 2, 0, 3), (31, 3, 1, 3),
    ],
    (2, 0): [
        (12, 4, 0, 0), (12, 4, 0, 2), (15, 0, 0, 0), (15, 0, 0, 2), (21, 0, 1, 2), (21, 1, 0, 0),
        (24, 1, 0, 2), (25, 0, 1, 0), (27, 3, 0, 0), (28, 3, 0, 2), (31, 2, 0, 0), (31, 3, 1, 2),
        (31, 1, 1, 0), (31, 1, 1, 2), (31, 2, 0, 2), (31, 3, 1, 0), (31, 2, 1, 2), (31, 2, 1, 0),
    ],
    (2, 1): [
        (21, 4, 0, 1), (21, 4, 0, 3), (21, 0, 0, 1), (21, 0, 0, 3), (25, 3, 0, 1), (27, 3, 0, 3),
        (27, 0, 1, 3), (29, 1, 0, 1), (30, 1, 0, 3), (31, 0, 1, 1), (31, 3, 1, 1), (31, 2, 0, 3),
        (31, 2, 0, 1), (31, 3, 1, 3), (31, 1, 1, 1), (31, 1, 1, 3), (31, 2, 1, 1), (31, 2, 1, 3),
    ],
    (3, 0): [
        (4, 4, 0, 2), (4, 0, 0, 2), (12, 0, 1, 2), (15, 1, 0, 2), (21, 4, 0, 0), (21, 3, 0, 2),
        (21, 0, 0, 0), (25, 1, 1, 2), (27, 3, 1, 2), (27, 1, 0, 0), (29, 2, 0, 2), (30, 3, 1, 0),
        (31, 0, 1, 0), (31, 3, 0, 0), (31, 2, 1, 2), (31, 2, 1, 0), (31, 2, 0, 0), (31, 1, 1, 0),
    ],
    (3, 1): [
        (12, 4, 0, 3), (15, 0, 0, 3), (18, 3, 0, 3), (21, 0, 1, 3), (23, 1, 0, 3), (28, 4, 0, 1),
        (29, 0, 0, 1), (30, 2, 0, 3), (31, 3, 0, 1), (31, 3, 1, 3), (31, 1, 1, 3), (31, 1, 0, 1),
        (31, 0, 1, 1), (31, 2, 1, 1), (31, 2, 1, 3), (31, 3, 1, 1), (31, 2, 0, 1), (31, 1, 1, 1),
    ],
}
BOTH = [(1, 1, 3), (2, 1, 0), (2, 1, 1), (2, 1, 2), (2, 1, 3), (3, 1, 0)]
QROWS = 384


RES = [(4, 0, 0), (4, 0, 2), (4, 0, 1), (4, 0, 3)]


def piece_index(piece):
    dx, dz, q = piece
    return (dx * 2 + dz) * 4 + q


def gather_kernel(dosage, missing, resid, rows_out, cols_out, res_out,
                  turned, own, stat_mine, stat_in,
                  stat_send, stat_recv, own_sem, row_send, row_recv,
                  chain_send, chip_send, other_send, col_recv):
    seg, row, col = lax.axis_index("segment"), lax.axis_index("row"), lax.axis_index("col")
    y, core = row // 2, row % 2
    x, zl = col // 2, col % 2
    samples = dosage.shape[1]
    col_of = lambda dx, dz: lax.rem(x + 4 - dx, 4) * 2 + lax.rem(zl + dz, 2)
    right = (seg, row, lax.rem(x + 1, 4) * 2 + zl)
    left = (seg, row, lax.rem(x + 3, 4) * 2 + zl)
    across = (seg, row, x * 2 + 1 - zl)
    up = (seg, lax.rem(y + 1, 4) * 2 + core, col)
    down = (seg, lax.rem(y + 3, 4) * 2 + core, col)
    mate = (seg, y * 2 + 1 - core, col)
    first = core == zl
    place = lax.rem(y + 4 - x, 4)
    source = first & (place == 0)
    helper = jnp.logical_not(first) & (place == 0)

    barrier = pltpu.get_barrier_semaphore()
    peers = [(seg, lax.rem(row + d, 8), col) for d in range(1, 8)] + [right, left, across]
    for peer in peers:
        pl.semaphore_signal(barrier, inc=1, device_id=peer, device_id_type=MESH_ID)

    def turn(j, sums):
        lanes = pl.ds(pl.multiple_of(j * 128, 128), 128)
        tile = jnp.where(missing[:, lanes] == 0, dosage[:, lanes], -1.0).T
        turned[lanes, :] = tile
        seen = (tile >= 0.0).astype(jnp.float32).reshape(16, 8, 128)
        alt = jnp.maximum(tile, 0.0).reshape(16, 8, 128)
        return sums[0] + jnp.sum(alt, axis=0), sums[1] + jnp.sum(seen, axis=0)

    zero = jnp.zeros((8, 128), jnp.float32)
    alt, seen = lax.fori_loop(0, samples // 128, turn, (zero, zero))
    which = lax.broadcasted_iota(jnp.int32, (8, 128), 0)
    stat_mine[...] = jnp.where(which == 0, jnp.sum(alt, axis=0, keepdims=True),
                               jnp.sum(seen, axis=0, keepdims=True))

    pl.semaphore_wait(barrier, len(peers))

    def piece_rows(q):
        return pl.ds(q * QROWS, QROWS)

    def col_ref(piece):
        dx, dz, q = piece
        if dx == 4:
            return res_out.at[piece_rows(q)]
        return cols_out.at[col_of(dx, dz), piece_rows(q)]

    def chain_copy(piece, src, q):
        return pltpu.make_async_remote_copy(
            src_ref=src, dst_ref=col_ref(piece),
            send_sem=chain_send.at[piece_index(piece)], recv_sem=col_recv.at[piece_index(piece)],
            device_id=up if q < 2 else down, device_id_type=MESH_ID)

    def other_copy(piece, src):
        return pltpu.make_async_remote_copy(
            src_ref=src, dst_ref=col_ref(piece),
            send_sem=other_send.at[BOTH.index(piece)], recv_sem=col_recv.at[piece_index(piece)],
            device_id=down if piece[2] < 2 else up, device_id_type=MESH_ID)

    def relays(piece, here):
        near = 1 if piece[2] < 2 else 3
        return here in ((0, near) if piece in BOTH else (0, near, 2))

    def chip_copy(piece, src):
        return pltpu.make_async_remote_copy(
            src_ref=src, dst_ref=col_ref(piece),
            send_sem=chip_send.at[piece_index(piece)], recv_sem=col_recv.at[piece_index(piece)],
            device_id=mate, device_id_type=MESH_ID)

    def from_source(piece):
        dx, dz, q = piece
        if dx == 4:
            src = resid.at[piece_rows(q)]
        else:
            here = (dx, dz) == (0, 0)
            src = own.at[piece_rows(q)] if here else rows_out.at[col_of(dx, dz), piece_rows(q)]

        @pl.when(source)
        def _():
            chip_copy(piece, src).start()
            if q % 2 == 0:
                chain_copy(piece, src, q).start()
                if piece in BOTH:
                    other_copy(piece, src).start()

    def stat_copy(d):
        return pltpu.make_async_remote_copy(
            src_ref=stat_mine, dst_ref=stat_in.at[d - 1],
            send_sem=stat_send.at[d - 1], recv_sem=stat_recv.at[d - 1],
            device_id=(seg, lax.rem(row + d, 8), col), device_id_type=MESH_ID)

    for d in range(1, 8):
        stat_copy(d).start()

    for piece in RES:
        from_source(piece)

    total = stat_mine[...]
    for d in range(1, 8):
        stat_copy(d).wait_recv()
        total = total + stat_in[d - 1]
    alt, seen = total[0:1], total[1:2]
    freq = (alt + 1.0) / (2.0 * seen + 2.0)
    twice = 2.0 * freq
    scale = 1.0 / jnp.sqrt(twice * (1.0 - freq))

    def row_copy(n, piece, target, rel):
        dx, dz, q = piece
        c = col_of(dx, dz)
        src = own.at[piece_rows(q)] if (dx, dz) == (0, 0) else rows_out.at[c, piece_rows(q)]
        return pltpu.make_async_remote_copy(
            src_ref=src, dst_ref=rows_out.at[c, piece_rows(q)],
            send_sem=row_send.at[n], recv_sem=row_recv.at[piece_index(rel)],
            device_id=target, device_id_type=MESH_ID)

    def row_arrival(piece):
        dx, dz, q = piece
        dst = rows_out.at[col_of(dx, dz), piece_rows(q)]
        return pltpu.make_async_remote_copy(
            src_ref=dst, dst_ref=dst, send_sem=row_send.at[0],
            recv_sem=row_recv.at[piece_index(piece)], device_id=right, device_id_type=MESH_ID)

    sends = []

    def send_row(piece, where):
        dx, dz, q = piece
        if where == "right":
            target, rel = right, ((dx + 1) % 4, dz, q)
        elif where == "left":
            target, rel = left, ((dx + 3) % 4, dz, q)
        else:
            target, rel = across, (dx, 1 - dz, q)
        copy = row_copy(len(sends), piece, target, rel)
        copy.start()
        sends.append(copy)

    def carrier(q):
        return first if q % 2 == 0 else jnp.logical_not(first)

    def pass_on(piece, here):
        q = piece[2]
        chip_copy(piece, col_ref(piece)).wait_recv()
        if relays(piece, here):
            chain_copy(piece, col_ref(piece), q).start()
        if here == 0 and piece in BOTH:
            other_copy(piece, col_ref(piece)).start()
        if here != 0:
            chip_copy(piece, col_ref(piece)).start()

    def standardize(q):
        def tile(t, _):
            part = pl.ds(pl.multiple_of(q * QROWS + t * 128, 128), 128)
            v = turned[part, :]
            own[part, :] = jnp.where(v >= 0.0, (v - twice) * scale, 0.0).astype(jnp.bfloat16)
            return 0
        lax.fori_loop(0, QROWS // 128, tile, 0, unroll=True)

    for piece in OWN:
        standardize(piece[2])
    for piece in OWN:
        q = piece[2]
        from_source(piece)
        send_row(piece, "right")
        send_row((0, 0, (1, 0, 3, 2)[q]), "left")
        send_row((0, 0, (2, 3, 0, 1)[q]), "across")
    keep = pltpu.make_async_copy(own, rows_out.at[col], own_sem)
    keep.start()

    order = RES + OWN + ARRIVE

    def chain_step(t):
        for (here, parity), steps in CHAIN.items():
            due = [tuple(entry[1:]) for entry in steps if entry[0] == t]
            if due:
                @pl.when(carrier(parity) & (place == here))
                def _(due=due, here=here):
                    for piece in due:
                        pass_on(piece, here)

    for i, piece in enumerate(ARRIVE):
        dx, dz, q = piece
        row_arrival(piece).wait_recv()
        if (dx, dz) == (0, 1) and q >= 2:
            send_row(piece, "right" if q == 2 else "left")
            send_row(piece, "left" if q == 2 else "right")
        if dx == 1 and q in (0, 2) and (dz == 0 or q == 2):
            send_row(piece, "right")
        if dx == 3 and q in (1, 3) and (dz == 0 or q == 3):
            send_row(piece, "left")
        if dz == 0 and q < 2:
            send_row(piece, "across")
        from_source(piece)
        chain_step(i + len(OWN))

    keep.wait()
    for copy in sends:
        copy.wait_send()
    for d in range(1, 8):
        stat_copy(d).wait_send()

    @pl.when(source)
    def _():
        for piece in order:
            chip_copy(piece, col_ref(piece)).wait_send()
            if piece[2] % 2 == 0:
                chain_copy(piece, col_ref(piece), piece[2]).wait_send()
                if piece in BOTH:
                    other_copy(piece, col_ref(piece)).wait_send()

    @pl.when(helper)
    def _():
        for piece in order:
            if piece[2] % 2 == 0:
                chip_copy(piece, col_ref(piece)).wait_recv()
            else:
                chain_copy(piece, col_ref(piece), piece[2]).wait_send()
                if piece in BOTH:
                    other_copy(piece, col_ref(piece)).wait_send()

    for q in range(4):
        mine = [piece for piece in order if piece[2] == q]
        @pl.when(carrier(q) & (place != 0))
        def _(mine=mine):
            for piece in mine:
                chip_copy(piece, col_ref(piece)).wait_send()

        for here in (1, 2, 3):
            @pl.when(carrier(q) & (place == here))
            def _(mine=mine, here=here):
                for piece in mine:
                    if relays(piece, here):
                        chain_copy(piece, col_ref(piece), piece[2]).wait_send()

        @pl.when(jnp.logical_not(carrier(q)) & (place != 0))
        def _(mine=mine):
            for piece in mine:
                chip_copy(piece, col_ref(piece)).wait_recv()


def gather(dosage, missing, residuals):
    variants, samples = dosage.shape
    tile = jax.ShapeDtypeStruct((8, samples, variants), jnp.bfloat16)
    vmem = pl.BlockSpec(memory_space=pltpu.VMEM)
    hbm = pl.BlockSpec(memory_space=pl.ANY)
    dma = pltpu.SemaphoreType.DMA
    return pl.pallas_call(
        gather_kernel,
        out_shape=(tile, tile, jax.ShapeDtypeStruct(residuals.shape, residuals.dtype)),
        in_specs=[vmem, vmem, hbm],
        out_specs=(hbm, hbm, hbm),
        scratch_shapes=[
            pltpu.VMEM((samples, variants), jnp.float32),
            pltpu.VMEM((samples, variants), jnp.bfloat16),
            pltpu.VMEM((8, 128), jnp.float32),
            pltpu.VMEM((7, 8, 128), jnp.float32),
            dma((7,)), dma((7,)), dma(()), dma((28,)), dma((32,)),
            dma((36,)), dma((36,)), dma((len(BOTH),)), dma((36,)),
        ],
        compiler_params=pltpu.CompilerParams(collective_id=1, has_side_effects=True),
        name="gather_genotypes",
    )(dosage, missing, residuals)


SLOTS = 5
SEGS = 6
DEPTH = 256
STEPS = 8
XO = (2, 1, 3, 0)


def scores_kernel(counts, rows_all, cols_all, grm_all, res_own, res_all, out,
                  rows, cols, wide, grm, res, acc, parts, from_x, from_z, mid_x, mid_z, last_z, last_x,
                  plan, load_sem, one_send, one_recv, two_send, two_recv):
    seg, row, col = (lax.axis_index(a) for a in ("segment", "row", "col"))
    x, zl = col // 2, col % 2
    z = seg * 2 + zl
    f32, bf16 = jnp.float32, jnp.bfloat16
    samples = cols.shape[1]
    shard = cols.shape[0] * cols.shape[2]
    chunk = samples // 4
    half = out.shape[1] // 2
    top, low = pl.ds(0, half), pl.ds(half, half)

    def at(to_x, to_z):
        return (to_z // 2, row, to_x * 2 + to_z % 2)

    def shifted(base, d):
        return lax.rem(base + d, 4)

    barrier = pltpu.get_barrier_semaphore()
    for d in (1, 2, 3):
        pl.semaphore_signal(barrier, inc=1, device_id=at(shifted(x, d), z), device_id_type=MESH_ID)
        pl.semaphore_signal(barrier, inc=1, device_id=at(x, shifted(z, d)), device_id_type=MESH_ID)

    def load(n, src, dst):
        return pltpu.make_async_copy(src, dst, load_sem.at[n])

    def chunk_rows(t):
        return pl.ds(pl.multiple_of(shifted(x, XO[t]) * chunk, chunk), chunk)

    def row_load(t):
        return load(2 + t, rows_all.at[:, chunk_rows(t)], rows.at[t])

    def grm_load(t):
        return load(6 + t, grm_all.at[chunk_rows(t)], grm.at[t])

    diagonal = row == col

    @pl.when(diagonal)
    def _():
        load(0, rows_all, cols).start()
        load(1, res_own, res).start()

    @pl.when(jnp.logical_not(diagonal))
    def _():
        load(0, cols_all, cols).start()
        load(1, res_all, res).start()

    for t in range(4):
        row_load(t).start()
        grm_load(t).start()

    flip = seg == 1
    sizes = [jnp.where(flip, counts[SEGS - 1 - i], counts[i]) for i in range(SLOTS)]
    ends, total = [], jnp.int32(0)
    for size in sizes:
        total = total + size
        ends.append(jnp.minimum(total, shard))
    pos, k = jnp.int32(0), jnp.int32(0)
    for j in range(STEPS):
        end, size = ends[SLOTS - 1], sizes[SLOTS - 1]
        for i in range(SLOTS - 2, -1, -1):
            end = jnp.where(k <= i, ends[i], end)
            size = jnp.where(k <= i, sizes[i], size)
        block = jnp.minimum(pos // DEPTH, shard // DEPTH - 1)
        stop = jnp.maximum(jnp.minimum(end, (block + 1) * DEPTH), pos)
        plan[0, j] = jnp.where(flip, shard // DEPTH - 1 - block, block)
        plan[1, j] = jnp.where(flip, shard - stop, pos)
        plan[2, j] = jnp.where(flip, shard - pos, stop)
        plan[3, j] = k
        plan[4, j] = size
        k = jnp.where(stop == end, k + 1, k)
        pos = stop

    load(0, cols_all, cols).wait()

    def widen(b, carry):
        wide[b, 0:128, :] = cols[2 * b].T
        wide[b, 128:256, :] = cols[2 * b + 1].T
        return carry

    lax.fori_loop(0, shard // DEPTH, widen, 0)
    load(1, res_all, res).wait()
    for t in range(4):
        row_load(t).wait()
    pl.semaphore_wait(barrier, 6)

    def compute(t, carry):
        acc[...] = jnp.zeros_like(acc)
        for j in range(STEPS):
            block, lower, upper = plan[0, j], plan[1, j], plan[2, j]
            left = jnp.concatenate([rows[t, 2 * block], rows[t, 2 * block + 1]], axis=1)
            variant = block * DEPTH + lax.broadcasted_iota(jnp.int32, left.shape, 1)
            left = jnp.where((variant >= lower) & (variant < upper), left, jnp.zeros_like(left))
            term = None
            for n in range(samples // 256):
                part = pl.ds(n * 256, 256)
                gram = jnp.dot(left, wide[block, :, part], preferred_element_type=f32)
                hadamard = (gram * grm[t, :, part].astype(f32)).astype(bf16)
                new = jnp.dot(hadamard, res[part, :], preferred_element_type=f32)
                term = new if term is None else term + new
            scale = 1.0 / jnp.full((1, 256), plan[4, j], jnp.int32).astype(f32)
            term = term * scale
            for k in range(max(0, j - 3), min(j, SLOTS - 1) + 1):
                acc[k] += jnp.where(plan[3, j] == k, term, 0.0)
        for k in range(SLOTS):
            for i in range(4):
                r = (i % 2) * 2 * half
                lanes = slice((i // 2) * 128, (i // 2) * 128 + 128)
                parts[t, i, k] = acc[k, r:r + 2 * half, lanes].astype(bf16)
        return carry

    def x_one(t, i):
        return pltpu.make_async_remote_copy(
            src_ref=parts.at[t, i, :, top], dst_ref=from_x.at[i, t],
            send_sem=one_send.at[0, t, i], recv_sem=one_recv.at[0, t, i],
            device_id=at(shifted(x, XO[t]), z), device_id_type=MESH_ID)

    def z_one(t, d):
        to_z = shifted(z, d)
        return pltpu.make_async_remote_copy(
            src_ref=parts.at[t, to_z, :, low], dst_ref=from_z.at[t, d - 1],
            send_sem=one_send.at[1, t, d], recv_sem=one_recv.at[1, t, d],
            device_id=at(x, to_z), device_id_type=MESH_ID)

    def x_two(d):
        to_z = shifted(z, d)
        return pltpu.make_async_remote_copy(
            src_ref=mid_x.at[to_z], dst_ref=last_z.at[d - 1],
            send_sem=two_send.at[0, d], recv_sem=two_recv.at[0, d],
            device_id=at(x, to_z), device_id_type=MESH_ID)

    def z_two(t):
        return pltpu.make_async_remote_copy(
            src_ref=mid_z.at[t], dst_ref=last_x.at[t],
            send_sem=two_send.at[1, t], recv_sem=two_recv.at[1, t],
            device_id=at(shifted(x, XO[t]), z), device_id_type=MESH_ID)

    def place_slots(write, mine, others):
        def go(near, far, seg_is):
            for s in range(SEGS):
                total = jnp.zeros((half, 128), f32)
                i = s if seg_is == 0 else SEGS - 1 - s
                if i < SLOTS:
                    total = total + (mine(i) + others(near, i))
                if SEGS - 1 - i < SLOTS:
                    total = total + (others(far, SEGS - 1 - i) + others(2, SEGS - 1 - i))
                write(s, total)

        for seg_is in (0, 1):
            for zl_is in (0, 1):
                near, far = (3, 1) if zl_is == 0 else (1, 3)

                @pl.when((seg == seg_is) & (zl == zl_is))
                def _(near=near, far=far, seg_is=seg_is):
                    go(near, far, seg_is)

    def low_sum(t):
        for d in (1, 2, 3):
            z_one(t, d).wait_recv()

        def write(s, total):
            mid_z[t, s] = total.astype(bf16)

        place_slots(write, lambda i: parts[t, z, i, low, :].astype(f32),
                    lambda d, i: from_z[t, d - 1, i].astype(f32))
        if XO[t] != 0:
            z_two(t).start()

    for t in range(4):
        grm_load(t).wait()
        compute(t, 0)
        for i in (1, 2, 3, 0):
            if XO[t] != 0:
                x_one(t, i).start()
        for d in (2, 1, 3):
            z_one(t, d).start()
        if t > 0:
            low_sum(t - 1)

    def top_sum(i):
        for t in range(3):
            x_one(t, i).wait_recv()
        for k in range(SLOTS):
            got = [from_x[i, t, k].astype(f32) for t in range(3)]
            total = (got[0] + got[1]) + (got[2] + parts[3, i, k, top, :].astype(f32))
            mid_x[i, k] = total.astype(bf16)

    for i in range(4):
        top_sum(i)
    for d in (2, 1, 3):
        x_two(d).start()
    low_sum(3)
    for t in range(3):
        z_two(t).wait_recv()
    for s in range(SEGS):
        got = [last_x[t, s].astype(f32) for t in range(3)]
        out[s, low] = ((got[0] + got[1]) + (got[2] + mid_z[3, s].astype(f32))).astype(bf16)
    for d in (1, 2, 3):
        x_two(d).wait_recv()

    def write(s, total):
        out[s, top] = total.astype(bf16)

    place_slots(write, lambda i: mid_x[z, i].astype(f32), lambda d, i: last_z[d - 1, i].astype(f32))

    for t in range(4):
        if XO[t] != 0:
            for i in range(4):
                x_one(t, i).wait_send()
            z_two(t).wait_send()
        for d in (1, 2, 3):
            z_one(t, d).wait_send()
    for d in (1, 2, 3):
        x_two(d).wait_send()


def scores(seg_counts, rows, cols, grm, res_own, res_all):
    samples = rows.shape[1]
    out_rows = samples // 8
    half = out_rows // 2
    bf16 = jnp.bfloat16
    dma = pltpu.SemaphoreType.DMA
    hbm = pl.BlockSpec(memory_space=pl.ANY)
    return pl.pallas_call(
        scores_kernel,
        out_shape=jax.ShapeDtypeStruct((SEGS, out_rows, 128), bf16),
        in_specs=[pl.BlockSpec(memory_space=pltpu.SMEM), hbm, hbm, hbm, hbm, hbm],
        out_specs=pl.BlockSpec(memory_space=pltpu.VMEM),
        scratch_shapes=[
            pltpu.VMEM((4, 8, samples // 4, 128), bf16),
            pltpu.VMEM((8, samples, 128), bf16),
            pltpu.VMEM((4, DEPTH, samples), bf16),
            pltpu.VMEM((4, samples // 4, samples), bf16),
            pltpu.VMEM(res_own.shape, bf16),
            pltpu.VMEM((SLOTS, samples // 4, 256), jnp.float32),
            pltpu.VMEM((4, 4, SLOTS, out_rows, 128), bf16),
            pltpu.VMEM((4, 3, SLOTS, half, 128), bf16),
            pltpu.VMEM((4, 3, SLOTS, half, 128), bf16),
            pltpu.VMEM((4, SLOTS, half, 128), bf16),
            pltpu.VMEM((4, SEGS, half, 128), bf16),
            pltpu.VMEM((3, SLOTS, half, 128), bf16),
            pltpu.VMEM((3, SEGS, half, 128), bf16),
            pltpu.SMEM((5, STEPS), jnp.int32),
            dma((10,)), dma((2, 4, 4)), dma((2, 4, 4)), dma((2, 4)), dma((2, 4)),
        ],
        compiler_params=pltpu.CompilerParams(
            vmem_limit_bytes=60 << 20, collective_id=2, has_side_effects=True),
        name="scores",
    )(seg_counts, rows, cols, grm, res_own, res_all)


def shards(dosage, missing, residuals, global_grm, seg_counts):
    rows, cols, res = gather(dosage, missing, residuals)
    return scores(seg_counts, rows, cols, global_grm, residuals, res)


def solution(mesh):
    placed = (
        P(("segment", "col"), "row"),
        P(("segment", "col"), "row"),
        P("row", None),
        P("row", "col"),
        P(),
    )
    return jax.shard_map(
        shards,
        mesh=mesh,
        in_specs=placed,
        out_specs=P(None, ("row", "col"), "segment"),
        check_vma=False,
    )
```
